32 devices in a mesh: tiles: 2 (over y), depth: 4 (over z), rows: 4 (over x, core).
Axes of the slice: x: 2, y: 2, z: 4, core: 2. Of those that a mesh axis runs over, the one named last changes fastest.
Arguments:
- volume: bfloat16 [32, 32, 32, 128], P(('tiles', 'depth'), 'rows'), parts along dimension 0, may hold values from -6 to 6
- prior: float32 [32, 32, 128], P(('tiles', 'depth'), 'rows'), parts along dimension 0, as said below
- first_kernel: bfloat16 [3, 3, 3, 32, 32], replicated, may hold values from -0.21875 to 0.21875
- second_kernel: bfloat16 [3, 3, 3, 32, 32], replicated, may hold values from -0.21875 to 0.21875
- projection: float32 [32], replicated, may hold values from -2 to 2
Outputs:
- joined: float32 [64, 32, 128], P(('tiles', 'rows')), parts along dimension 0
- depth_estimate: float32 [64, 128], P(('tiles', 'rows')), parts along dimension 0
The draws below stay inside these ranges and needn't reach their ends.
There are 2 independent parts, one for each index of `tiles`. The reference program is written for one: setup_inputs(seed, part) draws one part's arguments, and reference() takes and returns one part's arrays. A program takes and returns all parts, laid end to end along the dimension named above; an argument that names none is the same for every part. Nothing has to cross between parts.
Inputs may be any that keep to these rules, and one draw needn't show every extreme that they name: `prior`: finite real values.
All inputs are finite; a program needn't handle non-finite values.
Results may differ from the reference program's by a relative error of at most 0.0045.
Values may be sent and summed in bfloat16 or wider, within the bound.
No kernel may reach another device: no remote copies, remote signals or barrier semaphores. Data moves between devices by JAX's collectives and lax.ppermute only.
A program may use at most 64 MiB of HBM per device.

```python
import jax
import jax.numpy as jnp
from jax import lax

C = 32
WIDTH = 128
DEPTH = 16
HEIGHT = 32


def draw_prior(key, part):
    noise_key = jax.random.fold_in(key, 11)
    offset_key = jax.random.fold_in(key, 12)
    noise = jax.random.normal(noise_key, (DEPTH, HEIGHT, WIDTH), jnp.float32)
    offset = jax.random.uniform(offset_key, (HEIGHT, WIDTH), jnp.float32, -2.0, 2.0)
    return offset[None] + 2.0 * jnp.clip(noise, -6.0, 6.0)


def shard_levels(stream_key, shape, shards, least, high):
    def one(axis_at, blocks):
        heights = jax.random.uniform(jax.random.fold_in(jax.random.fold_in(stream_key, 6), axis_at), (blocks,), jnp.float32, least / len(shards), high / len(shards))
        return jnp.repeat(jnp.exp(heights), shape[axis_at] // blocks).reshape((-1,) + (1,) * (len(shape) - axis_at - 1))

    loudness = one(*shards[0])
    for cut in shards[1:]:
        loudness = loudness * one(*cut)
    return loudness


def bell_draw(key, shape, spread, reach, split=(), dtype=jnp.bfloat16):
    drawn = spread * jax.random.normal(key, shape, jnp.float32)
    if split:
        drawn = drawn * shard_levels(key, shape, split, -0.22, 0.18)
    return jnp.clip(drawn, -reach, reach).astype(dtype)


def setup_inputs(seed: int = 0, part: int = 0) -> dict:
    seeds = jax.random.split(jax.random.key(seed), 6)
    part_splits = jax.random.split(jax.random.fold_in(seeds[5], part), 6)
    return {
        "volume": bell_draw(part_splits[0], (DEPTH, HEIGHT, C, WIDTH), 1.0, 6.0, ((0, 4), (1, 4))),
        "prior": draw_prior(jax.random.fold_in(jax.random.fold_in(seeds[5], part), 71), part),
        "first_kernel": bell_draw(seeds[2], (3, 3, 3, C, C), (27 * C) ** -0.5, 0.21875),
        "second_kernel": bell_draw(seeds[3], (3, 3, 3, C, C), (27 * C) ** -0.5, 0.21875),
        "projection": bell_draw(seeds[4], (C,), (C // 4) ** -0.5, 2.0, (), jnp.float32),
    }


def convolve(field, kernel):
    result = lax.conv_general_dilated(field[None].astype(jnp.float32), kernel.astype(jnp.float32), (1, 1, 1), ((1, 1), (1, 1), (1, 1)), dimension_numbers=("NDHCW", "DHWIO", "NDHCW"), precision=lax.Precision.HIGHEST)[0]
    return jnp.maximum(result, 0.0).astype(jnp.bfloat16)


def reference(volume, prior, first_kernel, second_kernel, projection):
    first = convolve(volume, first_kernel)
    second = convolve(first, second_kernel)
    features = second.astype(jnp.float32)
    score = jnp.sum(features * projection[None, None, :, None], axis=2) + prior
    peak = jnp.max(score, axis=0)
    expd = jnp.exp(score - peak[None])
    total = jnp.sum(expd, axis=0)
    joined = jnp.einsum("dhw,dhcw->hcw", expd, features) / total[:, None, :]
    planes = (jnp.arange(DEPTH).astype(jnp.float32) + 0.5) / DEPTH
    depth_estimate = jnp.sum(expd * planes[:, None, None], axis=0) / total
    return joined, depth_estimate
```

```python
import functools

import jax
import jax.numpy as jnp
from jax import lax
from jax.experimental import pallas as pl
from jax.experimental.pallas import tpu as pltpu
from jax.sharding import PartitionSpec as P

F32 = jnp.float32
BF16 = jnp.bfloat16
AXES = ("depth", "rows")
VMEM = pl.BlockSpec(memory_space=pltpu.VMEM)


def exchange(value, shape, target):
    depth, rows = shape
    pairs = []
    for d in range(depth):
        for r in range(rows):
            to_d, to_r = target(d, r)
            if 0 <= to_d < depth and 0 <= to_r < rows:
                pairs.append((d * rows + r, to_d * rows + to_r))
    return lax.ppermute(value, AXES, pairs)


def prepare_kernel(k1_ref, k2_ref, proj_ref, w1_ref, w2_ref, pb_ref):
    taps = k1_ref.shape[0]
    chans = k1_ref.shape[3]
    span = taps * chans
    for k_ref, w_ref in ((k1_ref, w1_ref), (k2_ref, w2_ref)):
        made = w_ref.shape[0] // (taps * chans)
        for e in range(taps):
            flat = jnp.concatenate(
                [k_ref[a, b, e].astype(F32) for a in range(taps) for b in range(taps)]
                + [jnp.zeros(((made - 1) * span, chans), F32)],
                axis=0,
            )
            turned = flat.T
            for p in range(made):
                moved = turned if p == 0 else pltpu.roll(turned, p * span, 1)
                at = (e * made + p) * chans
                w_ref[at : at + chans, :] = moved.astype(BF16)
    lanes = pb_ref.shape[1]
    pb_ref[...] = jnp.broadcast_to(proj_ref[...], (lanes, chans)).T


def shifted_sum(y, group):
    width = y.shape[1] // 2
    lane = lax.broadcasted_iota(jnp.int32, (1, width), 1)
    parts = []
    for s in range(2):
        cols = slice(s * width, (s + 1) * width)
        before = pltpu.roll(y[:group, cols], 1, 1)
        here = y[group : 2 * group, cols]
        after = pltpu.roll(y[2 * group :, cols], width - 1, 1)
        parts.append(
            here + jnp.where(lane == 0, 0.0, before) + jnp.where(lane == width - 1, 0.0, after)
        )
    return parts


def pieces(value, count):
    out = []
    for _ in range(count - 1):
        top = value.astype(BF16).astype(F32)
        out.append(top)
        value = value - top
    return out + [value]


def store_parcel(ref, rows, feats, peak, total, depth):
    for i in range(rows):
        ref[i] = feats[i].astype(BF16)
    chans = ref.shape[1]
    flat = pieces(peak * 0.5, 3) + pieces(total, 2) + pieces(depth, 2)
    flat = flat + [jnp.zeros_like(peak)] * (-len(flat) % (chans // rows))
    per = chans // rows
    for j in range(0, len(flat), per):
        ref[rows + j // per] = jnp.concatenate(flat[j : j + per], axis=0).astype(BF16)


def load_stats(ref, rows):
    per = ref.shape[1] // rows
    flat = []
    for j in range(ref.shape[0] - rows):
        block = ref[rows + j].astype(F32)
        flat += [block[k * rows : (k + 1) * rows] for k in range(per)]
    peak = ((flat[0] + flat[1]) + flat[2]) * 2.0
    return peak, flat[3] + flat[4], flat[5] + flat[6]


def stat_blocks(rows, chans):
    per = chans // rows
    return -(-7 // per)


def volume_kernel(
    shape, own_ref, sib_ref, zh_ref, xt_ref, xb_ref, dt_ref, db_ref, op_ref, sp_ref, w1_ref,
    w2_ref, pb_ref, keep_ref, stat_ref, send_ref, xs_ref, fs_ref, ps_ref, ss_ref,
):
    depth, rows_axis = shape
    planes, rows, chans, width = own_ref.shape
    half = planes // 2
    halo = 2
    wide = 2 * width
    d = lax.axis_index("depth")
    r = lax.axis_index("rows")
    core = r % 2
    col = r // 2
    at_top = col == 0
    at_bottom = col == rows_axis // 2 - 1
    left = slice(0, width)
    right = slice(width, wide)
    zero_rows = jnp.zeros((planes, halo, chans, width), BF16)

    def fill(c):
        blocks = (own_ref, sib_ref) if c == 0 else (sib_ref, own_ref)
        base = halo * (1 - c)
        mine = slice(base, base + planes)
        zs = slice(0, halo) if c == 0 else slice(planes, planes + halo)
        n = rows + halo
        xs_ref[mine, halo:n, :, left] = blocks[0][...]
        xs_ref[mine, n:, :, left] = blocks[1][:, :halo]
        xs_ref[mine, :halo, :, right] = blocks[0][:, rows - halo :]
        xs_ref[mine, halo:n, :, right] = blocks[1][...]
        xs_ref[mine, :halo, :, left] = jnp.where(at_top, zero_rows, xt_ref[...])
        xs_ref[mine, n:, :, right] = jnp.where(at_bottom, zero_rows, xb_ref[...])
        xs_ref[zs, halo:, :, left] = zh_ref[:, :n]
        xs_ref[zs, :n, :, right] = zh_ref[:, rows - halo :]
        xs_ref[zs, :halo, :, left] = jnp.where(at_top, zero_rows[:halo], dt_ref[...])
        xs_ref[zs, n:, :, right] = jnp.where(at_bottom, zero_rows[:halo], db_ref[...])
        mine_p = slice(half * c, half * c + half)
        ps_ref[:, :, left] = (op_ref if c == 0 else sp_ref)[mine_p]
        ps_ref[:, :, right] = (sp_ref if c == 0 else op_ref)[mine_p]

    for c in range(2):
        pl.when(core == c)(functools.partial(fill, c))

    group = half * chans
    first_plane = d * planes + core * half - 1
    all_planes = depth * planes
    w1 = w1_ref[...]
    for g in range(0, half + 2, half):
        for i in range(rows + 2):
            x = xs_ref[g : g + half + 2, i : i + 3].reshape((half + 2) * 3 * chans, wide)
            y = jnp.dot(w1, x, preferred_element_type=F32)
            lo, hi = shifted_sum(y, group)
            lo = jnp.maximum(lo, 0.0)
            hi = jnp.maximum(hi, 0.0)
            if i == 0:
                lo = jnp.where(at_top, 0.0, lo)
            if i == rows + 1:
                hi = jnp.where(at_bottom, 0.0, hi)
            for p in range(half):
                part = slice(p * chans, (p + 1) * chans)
                a, b = lo[part], hi[part]
                if g + p == 0 or g + p == half + 1:
                    plane = first_plane + g + p
                    outside = jnp.logical_or(plane < 0, plane >= all_planes)
                    a = jnp.where(outside, 0.0, a)
                    b = jnp.where(outside, 0.0, b)
                fs_ref[g + p, i, :, left] = a.astype(BF16)
                fs_ref[g + p, i, :, right] = b.astype(BF16)

    w2 = w2_ref[...]
    pb = pb_ref[...]
    kept = core == 0
    fracs = [
        ((first_plane + 1 + p).astype(F32) + 0.5) / all_planes for p in range(half)
    ]
    for i in range(rows):
        x = fs_ref[:, i : i + 3].reshape((half + 2) * 3 * chans, wide)
        y = jnp.dot(w2, x, preferred_element_type=F32)
        sides = []
        for s, side in enumerate(shifted_sum(y, group)):
            cols = left if s == 0 else right
            side = jnp.maximum(side, 0.0).astype(BF16).astype(F32)
            feats = [side[p * chans : (p + 1) * chans] for p in range(half)]
            scores = [
                jnp.sum(feats[p] * pb, axis=0, keepdims=True) + ps_ref[p, i : i + 1, cols]
                for p in range(half)
            ]
            peak = functools.reduce(jnp.maximum, scores)
            weights = [jnp.exp(s_ - peak) for s_ in scores]
            total = functools.reduce(jnp.add, weights)
            depth_sum = functools.reduce(jnp.add, [w * f for w, f in zip(weights, fracs)])
            feat = functools.reduce(jnp.add, [w * f for w, f in zip(weights, feats)])
            sides.append((feat, peak, total, depth_sum))
        lo, hi = sides
        keep_ref[i] = jnp.where(kept, lo[0], hi[0])
        send_ref[i] = jnp.where(kept, hi[0], lo[0]).astype(BF16)
        for k in range(3):
            stat_ref[k, i : i + 1, :] = jnp.where(kept, lo[k + 1], hi[k + 1])
            ss_ref[k, i : i + 1, :] = jnp.where(kept, hi[k + 1], lo[k + 1])
    per = chans // rows
    flat = pieces(ss_ref[0] * 0.5, 3) + pieces(ss_ref[1], 2) + pieces(ss_ref[2], 2)
    flat = flat + [jnp.zeros_like(flat[0])] * (-len(flat) % per)
    for j in range(0, len(flat), per):
        send_ref[rows + j // per] = jnp.concatenate(flat[j : j + per], axis=0).astype(BF16)


def merge(one, two, rows):
    (feat_a, stats_a), (feat_b, stats_b) = one, two
    peak = jnp.maximum(stats_a[0], stats_b[0])
    wa = jnp.exp(stats_a[0] - peak)
    wb = jnp.exp(stats_b[0] - peak)
    total = wa * stats_a[1] + wb * stats_b[1]
    depth = wa * stats_a[2] + wb * stats_b[2]
    feats = [
        wa[i : i + 1] * feat_a(i) + wb[i : i + 1] * feat_b(i) for i in range(rows)
    ]
    return feats, peak, total, depth


def parcel(ref, rows):
    return (lambda i: ref[i].astype(F32)), load_stats(ref, rows)


def first_merge_kernel(keep_ref, stat_ref, got_ref, out_ref):
    rows = keep_ref.shape[0]
    mine = (lambda i: keep_ref[i]), tuple(stat_ref[k] for k in range(3))
    store_parcel(out_ref, rows, *merge(mine, parcel(got_ref, rows), rows))


def merge_kernel(step, own_ref, got_ref, out_ref):
    chans = own_ref.shape[1]
    rows = stat_ref_rows(own_ref.shape)
    low = (lax.axis_index("depth") // step) % 2 == 0

    def go(a_ref, b_ref):
        store_parcel(out_ref, rows, *merge(parcel(a_ref, rows), parcel(b_ref, rows), rows))

    pl.when(low)(lambda: go(own_ref, got_ref))
    pl.when(jnp.logical_not(low))(lambda: go(got_ref, own_ref))


def stat_ref_rows(shape):
    for rows in range(1, shape[0]):
        if rows + stat_blocks(rows, shape[1]) == shape[0]:
            return rows


def last_merge_kernel(step, own_ref, got_ref, joined_ref, depth_ref):
    rows = joined_ref.shape[0]
    low = (lax.axis_index("depth") // step) % 2 == 0

    def go(a_ref, b_ref):
        feats, _, total, depth = merge(parcel(a_ref, rows), parcel(b_ref, rows), rows)
        inverse = 1.0 / total
        for i in range(rows):
            joined_ref[i] = feats[i] * inverse[i : i + 1]
        depth_ref[...] = depth * inverse

    pl.when(low)(lambda: go(own_ref, got_ref))
    pl.when(jnp.logical_not(low))(lambda: go(got_ref, own_ref))


def call(kernel, outs, *args, scratch=(), flops=0, nbytes=0):
    return pl.pallas_call(
        kernel,
        out_shape=[jax.ShapeDtypeStruct(s, t) for s, t in outs],
        in_specs=[VMEM] * len(args),
        out_specs=[VMEM] * len(outs),
        scratch_shapes=list(scratch),
        cost_estimate=pl.CostEstimate(flops=flops, bytes_accessed=nbytes, transcendentals=0),
    )(*args)


def per_device(volume, prior, first_kernel, second_kernel, projection):
    planes, rows, chans, width = volume.shape
    depth, rows_axis = lax.axis_size("depth"), lax.axis_size("rows")
    shape = (depth, rows_axis)
    half = planes // 2
    halo = 2
    taps = first_kernel.shape[0]
    columns = rows_axis // 2
    assert half == halo and rows_axis % 2 == 0 and depth & (depth - 1) == 0 and chans % rows == 0

    def move(value, target):
        return exchange(value, shape, target)

    weight_shape = (taps * half * chans, (half + 2) * taps * chans)
    w1, w2, pb = call(
        prepare_kernel,
        [(weight_shape, BF16), (weight_shape, BF16), ((chans, width), F32)],
        first_kernel, second_kernel, projection[None, :],
        flops=10**8, nbytes=10**6,
    )

    core = lax.axis_index("rows") % 2
    col = lax.axis_index("rows") // 2
    lower = core == 0
    beside = move(volume, lambda d, r: (d, r ^ 1))
    prior_beside = move(prior, lambda d, r: (d, r ^ 1))

    top = jnp.where(lower, volume, beside)
    bottom = jnp.where(lower, beside, volume)
    edge = jnp.concatenate([top, bottom], axis=1)
    edge = jnp.where(lower, edge[:half], edge[half:])
    up = lambda d, r: (d + 1, r ^ 1) if r % 2 else (d - 1, r ^ 1)
    zh = move(edge, up)
    high = slice(0, halo)
    low = slice(rows - halo, rows)
    if columns == 2:
        first_col = col == 0
        pay = jnp.where(first_col, bottom[:, low], top[:, high])
        corner = jnp.where(lower, pay[:half], pay[half:])
        xt = xb = move(pay, lambda d, r: (d, r ^ 2))
        dt = db = move(corner, lambda d, r: (up(d, r)[0], r ^ 3))
    else:
        pays = bottom[:, low], top[:, high]
        corners = [jnp.where(lower, pay[:half], pay[half:]) for pay in pays]
        xt = move(pays[0], lambda d, r: (d, r + 2))
        xb = move(pays[1], lambda d, r: (d, r - 2))
        dt = move(corners[0], lambda d, r: (up(d, r)[0], (r ^ 1) + 2))
        db = move(corners[1], lambda d, r: (up(d, r)[0], (r ^ 1) - 2))

    parcel_shape = (rows + stat_blocks(rows, chans), chans, width)
    keep, stat, send = call(
        functools.partial(volume_kernel, shape),
        [((rows, chans, width), F32), ((3, rows, width), F32), (parcel_shape, BF16)],
        volume, beside, zh, xt, xb, dt, db, prior, prior_beside, w1, w2, pb,
        scratch=[
            pltpu.VMEM((planes + halo, rows + 2 * halo, chans, 2 * width), BF16),
            pltpu.VMEM((half + 2, rows + 2, chans, 2 * width), BF16),
            pltpu.VMEM((half, rows, 2 * width), F32),
            pltpu.VMEM((3, rows, width), F32),
        ],
        flops=10**9, nbytes=2 * 10**6,
    )
    got = move(send, lambda d, r: (d, r ^ 1))
    (sums,) = call(first_merge_kernel, [(parcel_shape, BF16)], keep, stat, got)
    step = 1
    while step < depth:
        got = move(sums, lambda d, r: (d ^ step, r))
        if 2 * step < depth:
            (sums,) = call(functools.partial(merge_kernel, step), [(parcel_shape, BF16)], sums, got)
        else:
            joined, depth_estimate = call(
                functools.partial(last_merge_kernel, step),
                [((rows, chans, width), F32), ((rows, width), F32)],
                sums, got,
            )
        step *= 2
    return joined, depth_estimate


def solution(mesh):
    placed = (
        P(("tiles", "depth"), "rows", None, None),
        P(("tiles", "depth"), "rows", None),
        P(),
        P(),
        P(),
    )
    return jax.shard_map(
        per_device,
        mesh=mesh,
        in_specs=placed,
        out_specs=(P(("tiles", "rows"), None, None), P(("tiles", "rows"), None)),
        check_vma=False,
    )
```

```python
import functools

import jax
import jax.numpy as jnp
from jax import lax
from jax.experimental import pallas as pl
from jax.experimental.pallas import tpu as pltpu
from jax.sharding import PartitionSpec as P

F32 = jnp.float32
BF16 = jnp.bfloat16
AXES = ("depth", "rows")
VMEM = pl.BlockSpec(memory_space=pltpu.VMEM)


def exchange(value, shape, target):
    depth, rows = shape
    pairs = []
    for d in range(depth):
        for r in range(rows):
            to_d, to_r = target(d, r)
            if 0 <= to_d < depth and 0 <= to_r < rows:
                pairs.append((d * rows + r, to_d * rows + to_r))
    return lax.ppermute(value, AXES, pairs)


def prepare_kernel(k1_ref, k2_ref, proj_ref, w1_ref, w2_ref, pb_ref):
    taps = k1_ref.shape[0]
    chans = k1_ref.shape[3]
    span = taps * chans
    for k_ref, w_ref in ((k1_ref, w1_ref), (k2_ref, w2_ref)):
        made = w_ref.shape[0] // (taps * chans)
        for e in range(taps):
            flat = jnp.concatenate(
                [k_ref[a, b, e].astype(F32) for a in range(taps) for b in range(taps)]
                + [jnp.zeros(((made - 1) * span, chans), F32)],
                axis=0,
            )
            turned = flat.T
            for p in range(made):
                moved = turned if p == 0 else pltpu.roll(turned, p * span, 1)
                at = (e * made + p) * chans
                w_ref[at : at + chans, :] = moved.astype(BF16)
    lanes = pb_ref.shape[1]
    pb_ref[...] = jnp.broadcast_to(proj_ref[...], (lanes, chans)).T


def shifted_sum(y, group):
    width = y.shape[1] // 2
    lane = lax.broadcasted_iota(jnp.int32, (1, width), 1)
    parts = []
    for s in range(2):
        cols = slice(s * width, (s + 1) * width)
        before = pltpu.roll(y[:group, cols], 1, 1)
        here = y[group : 2 * group, cols]
        after = pltpu.roll(y[2 * group :, cols], width - 1, 1)
        parts.append(
            here + jnp.where(lane == 0, 0.0, before) + jnp.where(lane == width - 1, 0.0, after)
        )
    return parts


def pieces(value, count):
    out = []
    for _ in range(count - 1):
        top = value.astype(BF16).astype(F32)
        out.append(top)
        value = value - top
    return out + [value]


def store_parcel(ref, rows, feats, peak, total, depth):
    for i in range(rows):
        ref[i] = feats[i].astype(BF16)
    chans = ref.shape[1]
    flat = pieces(peak * 0.5, 3) + pieces(total, 2) + pieces(depth, 2)
    flat = flat + [jnp.zeros_like(peak)] * (-len(flat) % (chans // rows))
    per = chans // rows
    for j in range(0, len(flat), per):
        ref[rows + j // per] = jnp.concatenate(flat[j : j + per], axis=0).astype(BF16)


def load_stats(ref, rows):
    per = ref.shape[1] // rows
    flat = []
    for j in range(ref.shape[0] - rows):
        block = ref[rows + j].astype(F32)
        flat += [block[k * rows : (k + 1) * rows] for k in range(per)]
    peak = ((flat[0] + flat[1]) + flat[2]) * 2.0
    return peak, flat[3] + flat[4], flat[5] + flat[6]


def stat_blocks(rows, chans):
    per = chans // rows
    return -(-7 // per)


def volume_kernel(
    shape, own_ref, sib_ref, zh_ref, xt_ref, xb_ref, dt_ref, db_ref, op_ref, sp_ref, w1_ref,
    w2_ref, pb_ref, keep_ref, stat_ref, send_ref, xs_ref, fs_ref, ps_ref, ss_ref,
):
    depth, rows_axis = shape
    planes, rows, chans, width = own_ref.shape
    half = planes // 2
    halo = 2
    wide = 2 * width
    d = lax.axis_index("depth")
    r = lax.axis_index("rows")
    core = r % 2
    col = r // 2
    at_top = col == 0
    at_bottom = col == rows_axis // 2 - 1
    left = slice(0, width)
    right = slice(width, wide)
    zero_rows = jnp.zeros((planes, halo, chans, width), BF16)

    def fill(c):
        blocks = (own_ref, sib_ref) if c == 0 else (sib_ref, own_ref)
        base = halo * (1 - c)
        mine = slice(base, base + planes)
        zs = slice(0, halo) if c == 0 else slice(planes, planes + halo)
        n = rows + halo
        xs_ref[mine, halo:n, :, left] = blocks[0][...]
        xs_ref[mine, n:, :, left] = blocks[1][:, :halo]
        xs_ref[mine, :halo, :, right] = blocks[0][:, rows - halo :]
        xs_ref[mine, halo:n, :, right] = blocks[1][...]
        xs_ref[mine, :halo, :, left] = jnp.where(at_top, zero_rows, xt_ref[...])
        xs_ref[mine, n:, :, right] = jnp.where(at_bottom, zero_rows, xb_ref[...])
        xs_ref[zs, halo:, :, left] = zh_ref[:, :n]
        xs_ref[zs, :n, :, right] = zh_ref[:, rows - halo :]
        xs_ref[zs, :halo, :, left] = jnp.where(at_top, zero_rows[:halo], dt_ref[...])
        xs_ref[zs, n:, :, right] = jnp.where(at_bottom, zero_rows[:halo], db_ref[...])
        mine_p = slice(half * c, half * c + half)
        ps_ref[:, :, left] = (op_ref if c == 0 else sp_ref)[mine_p]
        ps_ref[:, :, right] = (sp_ref if c == 0 else op_ref)[mine_p]

    for c in range(2):
        pl.when(core == c)(functools.partial(fill, c))

    group = half * chans
    first_plane = d * planes + core * half - 1
    all_planes = depth * planes
    w1 = w1_ref[...]
    for g in range(0, half + 2, half):
        for i in range(rows + 2):
            x = xs_ref[g : g + half + 2, i : i + 3].reshape((half + 2) * 3 * chans, wide)
            y = jnp.dot(w1, x, preferred_element_type=F32)
            lo, hi = shifted_sum(y, group)
            lo = jnp.maximum(lo, 0.0)
            hi = jnp.maximum(hi, 0.0)
            if i == 0:
                lo = jnp.where(at_top, 0.0, lo)
            if i == rows + 1:
                hi = jnp.where(at_bottom, 0.0, hi)
            for p in range(half):
                part = slice(p * chans, (p + 1) * chans)
                a, b = lo[part], hi[part]
                if g + p == 0 or g + p == half + 1:
                    plane = first_plane + g + p
                    outside = jnp.logical_or(plane < 0, plane >= all_planes)
                    a = jnp.where(outside, 0.0, a)
                    b = jnp.where(outside, 0.0, b)
                fs_ref[g + p, i, :, left] = a.astype(BF16)
                fs_ref[g + p, i, :, right] = b.astype(BF16)

    w2 = w2_ref[...]
    pb = pb_ref[...]
    kept = core == 0
    fracs = [
        ((first_plane + 1 + p).astype(F32) + 0.5) / all_planes for p in range(half)
    ]
    for i in range(rows):
        x = fs_ref[:, i : i + 3].reshape((half + 2) * 3 * chans, wide)
        y = jnp.dot(w2, x, preferred_element_type=F32)
        sides = []
        for s, side in enumerate(shifted_sum(y, group)):
            cols = left if s == 0 else right
            side = jnp.maximum(side, 0.0).astype(BF16).astype(F32)
            feats = [side[p * chans : (p + 1) * chans] for p in range(half)]
            scores = [
                jnp.sum(feats[p] * pb, axis=0, keepdims=True) + ps_ref[p, i : i + 1, cols]
                for p in range(half)
            ]
            peak = functools.reduce(jnp.maximum, scores)
            weights = [jnp.exp(s_ - peak) for s_ in scores]
            total = functools.reduce(jnp.add, weights)
            depth_sum = functools.reduce(jnp.add, [w * f for w, f in zip(weights, fracs)])
            feat = functools.reduce(jnp.add, [w * f for w, f in zip(weights, feats)])
            sides.append((feat, peak, total, depth_sum))
        lo, hi = sides
        keep_ref[i] = jnp.where(kept, lo[0], hi[0])
        send_ref[i] = jnp.where(kept, hi[0], lo[0]).astype(BF16)
        for k in range(3):
            stat_ref[k, i : i + 1, :] = jnp.where(kept, lo[k + 1], hi[k + 1])
            ss_ref[k, i : i + 1, :] = jnp.where(kept, hi[k + 1], lo[k + 1])
    per = chans // rows
    flat = pieces(ss_ref[0] * 0.5, 3) + pieces(ss_ref[1], 2) + pieces(ss_ref[2], 2)
    flat = flat + [jnp.zeros_like(flat[0])] * (-len(flat) % per)
    for j in range(0, len(flat), per):
        send_ref[rows + j // per] = jnp.concatenate(flat[j : j + per], axis=0).astype(BF16)


def merge(one, two, rows):
    (feat_a, stats_a), (feat_b, stats_b) = one, two
    peak = jnp.maximum(stats_a[0], stats_b[0])
    wa = jnp.exp(stats_a[0] - peak)
    wb = jnp.exp(stats_b[0] - peak)
    total = wa * stats_a[1] + wb * stats_b[1]
    depth = wa * stats_a[2] + wb * stats_b[2]
    feats = [
        wa[i : i + 1] * feat_a(i) + wb[i : i + 1] * feat_b(i) for i in range(rows)
    ]
    return feats, peak, total, depth


def parcel(ref, rows):
    return (lambda i: ref[i].astype(F32)), load_stats(ref, rows)


def first_merge_kernel(keep_ref, stat_ref, got_ref, out_ref):
    rows = keep_ref.shape[0]
    mine = (lambda i: keep_ref[i]), tuple(stat_ref[k] for k in range(3))
    store_parcel(out_ref, rows, *merge(mine, parcel(got_ref, rows), rows))


def merge_kernel(step, own_ref, got_ref, out_ref):
    chans = own_ref.shape[1]
    rows = stat_ref_rows(own_ref.shape)
    low = (lax.axis_index("depth") // step) % 2 == 0

    def go(a_ref, b_ref):
        store_parcel(out_ref, rows, *merge(parcel(a_ref, rows), parcel(b_ref, rows), rows))

    pl.when(low)(lambda: go(own_ref, got_ref))
    pl.when(jnp.logical_not(low))(lambda: go(got_ref, own_ref))


def stat_ref_rows(shape):
    for rows in range(1, shape[0]):
        if rows + stat_blocks(rows, shape[1]) == shape[0]:
            return rows


def last_merge_kernel(step, own_ref, got_ref, joined_ref, depth_ref):
    rows = joined_ref.shape[0]
    low = (lax.axis_index("depth") // step) % 2 == 0

    def go(a_ref, b_ref):
        feats, _, total, depth = merge(parcel(a_ref, rows), parcel(b_ref, rows), rows)
        inverse = 1.0 / total
        for i in range(rows):
            joined_ref[i] = feats[i] * inverse[i : i + 1]
        depth_ref[...] = depth * inverse

    pl.when(low)(lambda: go(own_ref, got_ref))
    pl.when(jnp.logical_not(low))(lambda: go(got_ref, own_ref))


def call(kernel, outs, *args, scratch=(), flops=0, nbytes=0, room=4):
    return pl.pallas_call(
        kernel,
        out_shape=[jax.ShapeDtypeStruct(s, t) for s, t in outs],
        in_specs=[VMEM] * len(args),
        out_specs=[VMEM] * len(outs),
        scratch_shapes=list(scratch),
        cost_estimate=pl.CostEstimate(flops=flops, bytes_accessed=nbytes, transcendentals=0),
        compiler_params=pltpu.CompilerParams(vmem_limit_bytes=room * 2**20),
    )(*args)


def per_device(volume, prior, first_kernel, second_kernel, projection):
    planes, rows, chans, width = volume.shape
    depth, rows_axis = lax.axis_size("depth"), lax.axis_size("rows")
    shape = (depth, rows_axis)
    half = planes // 2
    halo = 2
    taps = first_kernel.shape[0]
    columns = rows_axis // 2
    assert half == halo and rows_axis % 2 == 0 and depth & (depth - 1) == 0 and chans % rows == 0

    def move(value, target):
        return exchange(value, shape, target)

    weight_shape = (taps * half * chans, (half + 2) * taps * chans)
    w1, w2, pb = call(
        prepare_kernel,
        [(weight_shape, BF16), (weight_shape, BF16), ((chans, width), F32)],
        first_kernel, second_kernel, projection[None, :],
        flops=10**8, nbytes=10**6,
    )

    core = lax.axis_index("rows") % 2
    col = lax.axis_index("rows") // 2
    lower = core == 0
    beside = move(volume, lambda d, r: (d, r ^ 1))
    prior_beside = move(prior, lambda d, r: (d, r ^ 1))
    beside, prior_beside = lax.optimization_barrier((beside, prior_beside))

    high = slice(0, halo)
    low = slice(rows - halo, rows)

    def parts(block):
        picked = jnp.where(lower, block[:half], block[half:])
        return picked, block[:, high], block[:, low]

    own_pick, own_high, own_low = lax.optimization_barrier(parts(volume))
    sib_pick, sib_high, sib_low = parts(beside)
    edge = jnp.where(
        lower,
        jnp.concatenate([own_pick, sib_pick], axis=1),
        jnp.concatenate([sib_pick, own_pick], axis=1),
    )
    top_high = jnp.where(lower, own_high, sib_high)
    bottom_low = jnp.where(lower, sib_low, own_low)
    up = lambda d, r: (d + 1, r ^ 1) if r % 2 else (d - 1, r ^ 1)
    zh = move(edge, up)
    if columns == 2:
        first_col = col == 0
        pay = jnp.where(first_col, bottom_low, top_high)
        corner = jnp.where(lower, pay[:half], pay[half:])
        xt = xb = move(pay, lambda d, r: (d, r ^ 2))
        dt = db = move(corner, lambda d, r: (up(d, r)[0], r ^ 3))
    else:
        pays = bottom_low, top_high
        corners = [jnp.where(lower, pay[:half], pay[half:]) for pay in pays]
        xt = move(pays[0], lambda d, r: (d, r + 2))
        xb = move(pays[1], lambda d, r: (d, r - 2))
        dt = move(corners[0], lambda d, r: (up(d, r)[0], (r ^ 1) + 2))
        db = move(corners[1], lambda d, r: (up(d, r)[0], (r ^ 1) - 2))

    parcel_shape = (rows + stat_blocks(rows, chans), chans, width)
    keep, stat, send = call(
        functools.partial(volume_kernel, shape),
        [((rows, chans, width), F32), ((3, rows, width), F32), (parcel_shape, BF16)],
        volume, beside, zh, xt, xb, dt, db, prior, prior_beside, w1, w2, pb,
        scratch=[
            pltpu.VMEM((planes + halo, rows + 2 * halo, chans, 2 * width), BF16),
            pltpu.VMEM((half + 2, rows + 2, chans, 2 * width), BF16),
            pltpu.VMEM((half, rows, 2 * width), F32),
            pltpu.VMEM((3, rows, width), F32),
        ],
        flops=10**9, nbytes=2 * 10**6, room=12,
    )
    got = move(send, lambda d, r: (d, r ^ 1))
    (sums,) = call(first_merge_kernel, [(parcel_shape, BF16)], keep, stat, got)
    step = 1
    while step < depth:
        got = move(sums, lambda d, r: (d ^ step, r))
        if 2 * step < depth:
            (sums,) = call(functools.partial(merge_kernel, step), [(parcel_shape, BF16)], sums, got)
        else:
            joined, depth_estimate = call(
                functools.partial(last_merge_kernel, step),
                [((rows, chans, width), F32), ((rows, width), F32)],
                sums, got,
            )
        step *= 2
    return joined, depth_estimate


def solution(mesh):
    placed = (
        P(("tiles", "depth"), "rows", None, None),
        P(("tiles", "depth"), "rows", None),
        P(),
        P(),
        P(),
    )
    return jax.shard_map(
        per_device,
        mesh=mesh,
        in_specs=placed,
        out_specs=(P(("tiles", "rows"), None, None), P(("tiles", "rows"), None)),
        check_vma=False,
    )
```

```python
import functools

import jax
import jax.numpy as jnp
from jax import lax
from jax.experimental import pallas as pl
from jax.experimental.pallas import tpu as pltpu
from jax.sharding import PartitionSpec as P


F32 = jnp.float32
BF16 = jnp.bfloat16
AXES = ("depth", "rows")
VMEM = pl.BlockSpec(memory_space=pltpu.VMEM)


def exchange(value, shape, target):
    depth, rows = shape
    pairs = []
    for d in range(depth):
        for r in range(rows):
            to_d, to_r = target(d, r)
            if 0 <= to_d < depth and 0 <= to_r < rows:
                pairs.append((d * rows + r, to_d * rows + to_r))
    return lax.ppermute(value, AXES, pairs)


def prepare_kernel(k1_ref, k2_ref, proj_ref, w1_ref, w2_ref, pb_ref):
    taps = k1_ref.shape[0]
    chans = k1_ref.shape[3]
    span = taps * chans
    for k_ref, w_ref in ((k1_ref, w1_ref), (k2_ref, w2_ref)):
        made = w_ref.shape[0] // (taps * chans)
        for e in range(taps):
            flat = jnp.concatenate(
                [k_ref[a, b, e].astype(F32) for a in range(taps) for b in range(taps)]
                + [jnp.zeros(((made - 1) * span, chans), F32)],
                axis=0,
            )
            turned = flat.T
            for p in range(made):
                moved = turned if p == 0 else pltpu.roll(turned, p * span, 1)
                at = (e * made + p) * chans
                w_ref[at : at + chans, :] = moved.astype(BF16)
    lanes = pb_ref.shape[1]
    pb_ref[...] = jnp.broadcast_to(proj_ref[...], (lanes, chans)).T


def cut_kernel(block_ref, pick_ref, high_ref, low_ref):
    half, halo = pick_ref.shape[0], high_ref.shape[1]
    rows = block_ref.shape[1]
    core = lax.axis_index("rows") % 2
    pick_ref[...] = block_ref[pl.ds(core * half, half)]
    high_ref[...] = block_ref[:, :halo]
    low_ref[...] = block_ref[:, rows - halo :]


def shifted_sum(y, group):
    width = y.shape[1] // 2
    lane = lax.broadcasted_iota(jnp.int32, (1, width), 1)
    parts = []
    for s in range(2):
        cols = slice(s * width, (s + 1) * width)
        before = pltpu.roll(y[:group, cols], 1, 1)
        here = y[group : 2 * group, cols]
        after = pltpu.roll(y[2 * group :, cols], width - 1, 1)
        parts.append(
            here + jnp.where(lane == 0, 0.0, before) + jnp.where(lane == width - 1, 0.0, after)
        )
    return parts


def pieces(value, count):
    out = []
    for _ in range(count - 1):
        top = value.astype(BF16).astype(F32)
        out.append(top)
        value = value - top
    return out + [value]


def store_parcel(ref, rows, feats, peak, total, depth):
    for i in range(rows):
        ref[i] = feats[i].astype(BF16)
    chans = ref.shape[1]
    flat = pieces(peak * 0.5, 3) + pieces(total, 2) + pieces(depth, 2)
    flat = flat + [jnp.zeros_like(peak)] * (-len(flat) % (chans // rows))
    per = chans // rows
    for j in range(0, len(flat), per):
        ref[rows + j // per] = jnp.concatenate(flat[j : j + per], axis=0).astype(BF16)


def load_stats(ref, rows):
    per = ref.shape[1] // rows
    flat = []
    for j in range(ref.shape[0] - rows):
        block = ref[rows + j].astype(F32)
        flat += [block[k * rows : (k + 1) * rows] for k in range(per)]
    peak = ((flat[0] + flat[1]) + flat[2]) * 2.0
    return peak, flat[3] + flat[4], flat[5] + flat[6]


def stat_blocks(rows, chans):
    per = chans // rows
    return -(-7 // per)


def first_layer(w, x, half, chans, first_plane, g, all_planes, store):
    lo, hi = shifted_sum(jnp.dot(w, x, preferred_element_type=F32), half * chans)
    for p in range(half):
        part = slice(p * chans, (p + 1) * chans)
        a, b = jnp.maximum(lo[part], 0.0), jnp.maximum(hi[part], 0.0)
        if g + p == 0 or g + p == half + 1:
            plane = first_plane + g + p
            outside = jnp.logical_or(plane < 0, plane >= all_planes)
            a = jnp.where(outside, 0.0, a)
            b = jnp.where(outside, 0.0, b)
        store(g + p, a, b)


def second_layer(w, x, pb, prior_row, fracs, half, chans):
    y = jnp.dot(w, x, preferred_element_type=F32)
    sides = []
    for s, side in enumerate(shifted_sum(y, half * chans)):
        side = jnp.maximum(side, 0.0).astype(BF16).astype(F32)
        feats = [side[p * chans : (p + 1) * chans] for p in range(half)]
        scores = [
            jnp.sum(feats[p] * pb, axis=0, keepdims=True) + prior_row(p, s) for p in range(half)
        ]
        peak = functools.reduce(jnp.maximum, scores)
        weights = [jnp.exp(s_ - peak) for s_ in scores]
        total = functools.reduce(jnp.add, weights)
        depth_sum = functools.reduce(jnp.add, [w_ * f for w_, f in zip(weights, fracs)])
        feat = functools.reduce(jnp.add, [w_ * f for w_, f in zip(weights, feats)])
        sides.append((feat, peak, total, depth_sum))
    return sides


def place_of(depth, planes):
    half = planes // 2
    core = lax.axis_index("rows") % 2
    first_plane = lax.axis_index("depth") * planes + core * half - 1
    all_planes = depth * planes
    fracs = [((first_plane + 1 + p).astype(F32) + 0.5) / all_planes for p in range(half)]
    return core, first_plane, all_planes, fracs


def inner_kernel(
    depth, own_ref, sib_ref, zh_ref, op_ref, sp_ref, w1_ref, w2_ref, pb_ref,
    xs_ref, fs_ref, ps_ref, keep_ref, send_ref, stat_ref, ss_ref,
):
    planes, rows, chans, width = own_ref.shape
    half = planes // 2
    halo = 2
    wide = 2 * width
    core, first_plane, all_planes, fracs = place_of(depth, planes)
    left = slice(0, width)
    right = slice(width, wide)
    n = rows + halo

    def fill(c):
        blocks = (own_ref, sib_ref) if c == 0 else (sib_ref, own_ref)
        base = halo * (1 - c)
        mine = slice(base, base + planes)
        zs = slice(0, halo) if c == 0 else slice(planes, planes + halo)
        xs_ref[mine, halo:n, :, left] = blocks[0][...]
        xs_ref[mine, n:, :, left] = blocks[1][:, :halo]
        xs_ref[mine, :halo, :, right] = blocks[0][:, rows - halo :]
        xs_ref[mine, halo:n, :, right] = blocks[1][...]
        xs_ref[zs, halo:, :, left] = zh_ref[:, :n]
        xs_ref[zs, :n, :, right] = zh_ref[:, rows - halo :]
        mine_p = slice(half * c, half * c + half)
        ps_ref[:, :, left] = (op_ref if c == 0 else sp_ref)[mine_p]
        ps_ref[:, :, right] = (sp_ref if c == 0 else op_ref)[mine_p]

    for c in range(2):
        pl.when(core == c)(functools.partial(fill, c))

    deep = (half + 2) * 3 * chans
    w1 = w1_ref[...]
    for g in range(0, half + 2, half):
        for i in range(halo, rows):
            def store(j, a, b, i=i):
                fs_ref[j, i - halo, :, left] = a.astype(BF16)
                fs_ref[j, i - halo, :, right] = b.astype(BF16)

            x = xs_ref[g : g + half + 2, i : i + 3].reshape(deep, wide)
            first_layer(w1, x, half, chans, first_plane, g, all_planes, store)

    w2 = w2_ref[...]
    pb = pb_ref[...]
    kept = core == 0
    for i in range(halo, rows - halo):
        x = fs_ref[:, i - halo : i - halo + 3].reshape(deep, wide)
        prior_row = lambda p, s: ps_ref[p, i : i + 1, right if s else left]
        lo, hi = second_layer(w2, x, pb, prior_row, fracs, half, chans)
        keep_ref[i - halo] = jnp.where(kept, lo[0], hi[0])
        send_ref[i - halo] = jnp.where(kept, hi[0], lo[0]).astype(BF16)
        for k in range(3):
            stat_ref[k, i : i + 1, :] = jnp.where(kept, lo[k + 1], hi[k + 1])
            ss_ref[k, i : i + 1, :] = jnp.where(kept, hi[k + 1], lo[k + 1])


def outer_kernel(
    shape, xt_ref, xb_ref, dt_ref, db_ref, xs_ref, fi_ref, ps_ref, ki_ref, si_ref, ti_ref, ui_ref,
    w1_ref, w2_ref, pb_ref, keep_ref, stat_ref, send_ref, top_ref, bottom_ref, fs_ref, ss_ref,
):
    depth, rows_axis = shape
    planes, halo, chans, width = xt_ref.shape
    half = planes // 2
    rows = keep_ref.shape[0]
    core, first_plane, all_planes, fracs = place_of(depth, planes)
    col = lax.axis_index("rows") // 2
    at_top = col == 0
    at_bottom = col == rows_axis // 2 - 1
    left = slice(0, width)
    right = slice(width, 2 * width)
    zero_rows = jnp.zeros((planes, halo, chans, width), BF16)

    def fill(c):
        base = halo * (1 - c)
        mine = slice(base, base + planes)
        zs = slice(0, halo) if c == 0 else slice(planes, planes + halo)
        top_ref[mine] = jnp.where(at_top, zero_rows, xt_ref[...])
        bottom_ref[mine] = jnp.where(at_bottom, zero_rows, xb_ref[...])
        top_ref[zs] = jnp.where(at_top, zero_rows[:halo], dt_ref[...])
        bottom_ref[zs] = jnp.where(at_bottom, zero_rows[:halo], db_ref[...])

    for c in range(2):
        pl.when(core == c)(functools.partial(fill, c))

    deep = (half + 2) * 3 * chans
    last = rows + 2
    w1 = w1_ref[...]
    for g in range(0, half + 2, half):
        span = slice(g, g + half + 2)
        for i in (0, 1, rows, rows + 1):
            if i < halo:
                lhs = jnp.concatenate(
                    [top_ref[span, i:], xs_ref[span, halo : i + 3, :, left]], axis=1
                )
                rhs = xs_ref[span, i : i + 3, :, right]
            else:
                lhs = xs_ref[span, i : i + 3, :, left]
                rhs = jnp.concatenate(
                    [xs_ref[span, i:last, :, right], bottom_ref[span, : i + 3 - last]], axis=1
                )
            x = jnp.concatenate([lhs.reshape(deep, width), rhs.reshape(deep, width)], axis=1)

            def store(j, a, b, i=i):
                if i == 0:
                    a = jnp.where(at_top, 0.0, a)
                if i == rows + 1:
                    b = jnp.where(at_bottom, 0.0, b)
                at = i if i < halo else i - rows + halo
                fs_ref[j, at, :, left] = a.astype(BF16)
                fs_ref[j, at, :, right] = b.astype(BF16)

            first_layer(w1, x, half, chans, first_plane, g, all_planes, store)

    w2 = w2_ref[...]
    pb = pb_ref[...]
    kept = core == 0
    inner = slice(halo, rows - halo)
    keep_ref[inner] = ki_ref[...]
    send_ref[inner] = si_ref[...]
    stat_ref[:, inner] = ti_ref[:, inner]
    ss_ref[:, inner] = ui_ref[:, inner]
    for i in (0, 1, rows - 2, rows - 1):
        if i < halo:
            x = jnp.concatenate([fs_ref[:, i:halo], fi_ref[:, : i + 3 - halo]], axis=1)
        else:
            x = jnp.concatenate([fi_ref[:, i - halo :], fs_ref[:, halo : i + 3 - rows + halo]], axis=1)
        prior_row = lambda p, s: ps_ref[p, i : i + 1, right if s else left]
        lo, hi = second_layer(w2, x.reshape(deep, 2 * width), pb, prior_row, fracs, half, chans)
        keep_ref[i] = jnp.where(kept, lo[0], hi[0])
        send_ref[i] = jnp.where(kept, hi[0], lo[0]).astype(BF16)
        for k in range(3):
            stat_ref[k, i : i + 1, :] = jnp.where(kept, lo[k + 1], hi[k + 1])
            ss_ref[k, i : i + 1, :] = jnp.where(kept, hi[k + 1], lo[k + 1])
    per = chans // rows
    flat = pieces(ss_ref[0] * 0.5, 3) + pieces(ss_ref[1], 2) + pieces(ss_ref[2], 2)
    flat = flat + [jnp.zeros_like(flat[0])] * (-len(flat) % per)
    for j in range(0, len(flat), per):
        send_ref[rows + j // per] = jnp.concatenate(flat[j : j + per], axis=0).astype(BF16)


def merge(one, two, rows):
    (feat_a, stats_a), (feat_b, stats_b) = one, two
    peak = jnp.maximum(stats_a[0], stats_b[0])
    wa = jnp.exp(stats_a[0] - peak)
    wb = jnp.exp(stats_b[0] - peak)
    total = wa * stats_a[1] + wb * stats_b[1]
    depth = wa * stats_a[2] + wb * stats_b[2]
    feats = [
        wa[i : i + 1] * feat_a(i) + wb[i : i + 1] * feat_b(i) for i in range(rows)
    ]
    return feats, peak, total, depth


def parcel(ref, rows):
    return (lambda i: ref[i].astype(F32)), load_stats(ref, rows)


def first_merge_kernel(keep_ref, stat_ref, got_ref, out_ref):
    rows = keep_ref.shape[0]
    mine = (lambda i: keep_ref[i]), tuple(stat_ref[k] for k in range(3))
    store_parcel(out_ref, rows, *merge(mine, parcel(got_ref, rows), rows))


def merge_kernel(step, own_ref, got_ref, out_ref):
    rows = stat_ref_rows(own_ref.shape)
    low = (lax.axis_index("depth") // step) % 2 == 0

    def go(a_ref, b_ref):
        store_parcel(out_ref, rows, *merge(parcel(a_ref, rows), parcel(b_ref, rows), rows))

    pl.when(low)(lambda: go(own_ref, got_ref))
    pl.when(jnp.logical_not(low))(lambda: go(got_ref, own_ref))


def stat_ref_rows(shape):
    for rows in range(1, shape[0]):
        if rows + stat_blocks(rows, shape[1]) == shape[0]:
            return rows


def last_merge_kernel(step, own_ref, got_ref, joined_ref, depth_ref):
    rows = joined_ref.shape[0]
    low = (lax.axis_index("depth") // step) % 2 == 0

    def go(a_ref, b_ref):
        feats, _, total, depth = merge(parcel(a_ref, rows), parcel(b_ref, rows), rows)
        inverse = 1.0 / total
        for i in range(rows):
            joined_ref[i] = feats[i] * inverse[i : i + 1]
        depth_ref[...] = depth * inverse

    pl.when(low)(lambda: go(own_ref, got_ref))
    pl.when(jnp.logical_not(low))(lambda: go(got_ref, own_ref))


def call(kernel, outs, *args, scratch=(), flops=0, nbytes=0, room=4):
    return pl.pallas_call(
        kernel,
        out_shape=[jax.ShapeDtypeStruct(s, t) for s, t in outs],
        in_specs=[VMEM] * len(args),
        out_specs=[VMEM] * len(outs),
        scratch_shapes=list(scratch),
        cost_estimate=pl.CostEstimate(flops=flops, bytes_accessed=nbytes, transcendentals=0),
        compiler_params=pltpu.CompilerParams(vmem_limit_bytes=room * 2**20),
    )(*args)


def body(volume, prior, first_kernel, second_kernel, projection):
    planes, rows, chans, width = volume.shape
    depth, rows_axis = lax.axis_size("depth"), lax.axis_size("rows")
    shape = (depth, rows_axis)
    half = planes // 2
    halo = 2
    taps = first_kernel.shape[0]
    columns = rows_axis // 2
    assert half == halo and rows_axis % 2 == 0 and depth & (depth - 1) == 0 and chans % rows == 0

    def move(value, target):
        return exchange(value, shape, target)

    weight_shape = (taps * half * chans, (half + 2) * taps * chans)
    w1, w2, pb = call(
        prepare_kernel,
        [(weight_shape, BF16), (weight_shape, BF16), ((chans, width), F32)],
        first_kernel, second_kernel, projection[None, :],
        flops=10**8, nbytes=10**6,
    )

    core = lax.axis_index("rows") % 2
    col = lax.axis_index("rows") // 2
    lower = core == 0
    beside = move(volume, lambda d, r: (d, r ^ 1))
    prior_beside = move(prior, lambda d, r: (d, r ^ 1))
    beside, prior_beside = lax.optimization_barrier((beside, prior_beside))

    high = slice(0, halo)
    low = slice(rows - halo, rows)

    def parts(block):
        picked = jnp.where(lower, block[:half], block[half:])
        return picked, block[:, high], block[:, low]

    edge_shape = (planes, halo, chans, width)
    own_pick, own_high, own_low = call(
        cut_kernel,
        [((half, rows, chans, width), BF16), (edge_shape, BF16), (edge_shape, BF16)],
        volume,
    )
    sib_pick, sib_high, sib_low = parts(beside)
    edge = jnp.where(
        lower,
        jnp.concatenate([own_pick, sib_pick], axis=1),
        jnp.concatenate([sib_pick, own_pick], axis=1),
    )
    top_high = jnp.where(lower, own_high, sib_high)
    bottom_low = jnp.where(lower, sib_low, own_low)
    up = lambda d, r: (d + 1, r ^ 1) if r % 2 else (d - 1, r ^ 1)
    zh = move(edge, up)
    if columns == 2:
        first_col = col == 0
        pay = jnp.where(first_col, bottom_low, top_high)
        corner = jnp.where(lower, pay[:half], pay[half:])
        xt = xb = move(pay, lambda d, r: (d, r ^ 2))
        dt = db = move(corner, lambda d, r: (up(d, r)[0], r ^ 3))
    else:
        pays = bottom_low, top_high
        corners = [jnp.where(lower, pay[:half], pay[half:]) for pay in pays]
        xt = move(pays[0], lambda d, r: (d, r + 2))
        xb = move(pays[1], lambda d, r: (d, r - 2))
        dt = move(corners[0], lambda d, r: (up(d, r)[0], (r ^ 1) + 2))
        db = move(corners[1], lambda d, r: (up(d, r)[0], (r ^ 1) - 2))

    parcel_shape = (rows + stat_blocks(rows, chans), chans, width)
    between = rows - 2 * halo
    stats_shape = (3, rows, width)
    inside = call(
        functools.partial(inner_kernel, depth),
        [
            ((planes + halo, rows + 2 * halo, chans, 2 * width), BF16),
            ((half + 2, rows - halo, chans, 2 * width), BF16),
            ((half, rows, 2 * width), F32),
            ((between, chans, width), F32),
            ((between, chans, width), BF16),
            (stats_shape, F32),
            (stats_shape, F32),
        ],
        volume, beside, zh, prior, prior_beside, w1, w2, pb,
        flops=5 * 10**8, nbytes=10**6, room=6,
    )
    keep, stat, send = call(
        functools.partial(outer_kernel, shape),
        [((rows, chans, width), F32), (stats_shape, F32), (parcel_shape, BF16)],
        xt, xb, dt, db, *inside, w1, w2, pb,
        scratch=[
            pltpu.VMEM((planes + halo, halo, chans, width), BF16),
            pltpu.VMEM((planes + halo, halo, chans, width), BF16),
            pltpu.VMEM((half + 2, 2 * halo, chans, 2 * width), BF16),
            pltpu.VMEM(stats_shape, F32),
        ],
        flops=5 * 10**8, nbytes=10**6, room=6,
    )
    got = move(send, lambda d, r: (d, r ^ 1))
    (sums,) = call(first_merge_kernel, [(parcel_shape, BF16)], keep, stat, got)
    step = 1
    while step < depth:
        got = move(sums, lambda d, r: (d ^ step, r))
        if 2 * step < depth:
            (sums,) = call(functools.partial(merge_kernel, step), [(parcel_shape, BF16)], sums, got)
        else:
            joined, depth_estimate = call(
                functools.partial(last_merge_kernel, step),
                [((rows, chans, width), F32), ((rows, width), F32)],
                sums, got,
            )
        step *= 2
    return joined, depth_estimate


def solution(mesh):
    placed = (
        P(("tiles", "depth"), "rows", None, None),
        P(("tiles", "depth"), "rows", None),
        P(),
        P(),
        P(),
    )
    return jax.shard_map(
        body,
        mesh=mesh,
        in_specs=placed,
        out_specs=(P(("tiles", "rows"), None, None), P(("tiles", "rows"), None)),
        check_vma=False,
    )
```

```python
import functools

import jax
import jax.numpy as jnp
from jax import lax
from jax.experimental import pallas as pl
from jax.experimental.pallas import tpu as pltpu
from jax.sharding import PartitionSpec as P


F32 = jnp.float32
BF16 = jnp.bfloat16
AXES = ("depth", "rows")
VMEM = pl.BlockSpec(memory_space=pltpu.VMEM)


def exchange(value, shape, target):
    depth, rows = shape
    pairs = []
    for d in range(depth):
        for r in range(rows):
            to_d, to_r = target(d, r)
            if 0 <= to_d < depth and 0 <= to_r < rows:
                pairs.append((d * rows + r, to_d * rows + to_r))
    return lax.ppermute(value, AXES, pairs)


def prepare_kernel(k1_ref, k2_ref, proj_ref, w1_ref, w2_ref, pb_ref):
    taps = k1_ref.shape[0]
    chans = k1_ref.shape[3]
    span = taps * chans
    turned_over = lax.axis_index("rows") // 2 == 1
    row_tap = [jnp.where(turned_over, taps - 1 - b, b) for b in range(taps)]
    for k_ref, w_ref in ((k1_ref, w1_ref), (k2_ref, w2_ref)):
        made = w_ref.shape[0] // (taps * chans)
        for e in range(taps):
            flat = jnp.concatenate(
                [k_ref[a, row_tap[b], e].astype(F32) for a in range(taps) for b in range(taps)]
                + [jnp.zeros(((made - 1) * span, chans), F32)],
                axis=0,
            )
            turned = flat.T
            for p in range(made):
                moved = turned if p == 0 else pltpu.roll(turned, p * span, 1)
                at = (e * made + p) * chans
                w_ref[at : at + chans, :] = moved.astype(BF16)
    lanes = pb_ref.shape[1]
    pb_ref[...] = jnp.broadcast_to(proj_ref[...], (lanes, chans)).T


def cut_kernel(block_ref, pick_ref, high_ref, low_ref):
    half, halo = pick_ref.shape[0], high_ref.shape[1]
    rows = block_ref.shape[1]
    core = lax.axis_index("rows") % 2
    pick_ref[...] = block_ref[pl.ds(core * half, half)]
    high_ref[...] = block_ref[:, :halo]
    low_ref[...] = block_ref[:, rows - halo :]


def shifted_sum(y, group):
    width = y.shape[1] // 2
    lane = lax.broadcasted_iota(jnp.int32, (1, width), 1)
    parts = []
    for s in range(2):
        cols = slice(s * width, (s + 1) * width)
        before = pltpu.roll(y[:group, cols], 1, 1)
        here = y[group : 2 * group, cols]
        after = pltpu.roll(y[2 * group :, cols], width - 1, 1)
        parts.append(
            here + jnp.where(lane == 0, 0.0, before) + jnp.where(lane == width - 1, 0.0, after)
        )
    return parts


def pieces(value, count):
    out = []
    for _ in range(count - 1):
        top = value.astype(BF16).astype(F32)
        out.append(top)
        value = value - top
    return out + [value]


def stat_pieces(peak, total, depth):
    return pieces(peak * 0.5, 3) + pieces(total, 2) + [depth]


def store_parcel(ref, feats, peak, total, depth):
    chans = feats[0].shape[0]
    for i, feat in enumerate(feats):
        ref[i * chans : (i + 1) * chans] = feat.astype(BF16)
    flat = stat_pieces(peak, total, depth)
    ref[len(feats) * chans :] = jnp.concatenate(flat, axis=0).astype(BF16)


def load_stats(ref, rows):
    flat = ref[ref.shape[0] - 6 * rows :].astype(F32)
    flat = [flat[k * rows : (k + 1) * rows] for k in range(6)]
    return ((flat[0] + flat[1]) + flat[2]) * 2.0, flat[3] + flat[4], flat[5]


def first_layer(w, x, half, chans, first_plane, g, all_planes, store):
    lo, hi = shifted_sum(jnp.dot(w, x, preferred_element_type=F32), half * chans)
    for p in range(half):
        part = slice(p * chans, (p + 1) * chans)
        a, b = jnp.maximum(lo[part], 0.0), jnp.maximum(hi[part], 0.0)
        if g + p == 0 or g + p == half + 1:
            plane = first_plane + g + p
            outside = jnp.logical_or(plane < 0, plane >= all_planes)
            a = jnp.where(outside, 0.0, a)
            b = jnp.where(outside, 0.0, b)
        store(g + p, a.astype(BF16), b.astype(BF16))


def second_layer(w, x, pb, ps_ref, fracs, two_rows, over, feat_ref, stat_ref):
    chans = feat_ref.shape[2]
    rows = feat_ref.shape[1]
    half = len(fracs)
    y = jnp.dot(w, x, preferred_element_type=F32)
    for row, side in zip(two_rows, shifted_sum(y, half * chans)):
        far = row // rows
        at = jnp.where(over, rows - 1 - row % rows, row % rows)
        side = jnp.maximum(side, 0.0).astype(BF16).astype(F32)
        feats = [side[p * chans : (p + 1) * chans] for p in range(half)]
        scores = [
            jnp.sum(feats[p] * pb, axis=0, keepdims=True) + ps_ref[far, p, pl.ds(at, 1), :]
            for p in range(half)
        ]
        peak = functools.reduce(jnp.maximum, scores)
        weights = [jnp.exp(s_ - peak) for s_ in scores]
        total = functools.reduce(jnp.add, weights)
        depth_sum = functools.reduce(jnp.add, [w_ * f for w_, f in zip(weights, fracs)])
        feat_ref[far, at] = functools.reduce(jnp.add, [w_ * f for w_, f in zip(weights, feats)])
        for k, value in enumerate((peak, total, depth_sum)):
            stat_ref[far, k, pl.ds(at, 1), :] = value


def place_of(depth, planes):
    half = planes // 2
    core = lax.axis_index("rows") % 2
    over = lax.axis_index("rows") // 2 == 1
    first_plane = lax.axis_index("depth") * planes + core * half - 1
    all_planes = depth * planes
    fracs = [((first_plane + 1 + p).astype(F32) + 0.5) / all_planes for p in range(half)]
    return core, over, first_plane, all_planes, fracs


def inner_kernel(
    depth, own_ref, sib_ref, zh_ref, op_ref, sp_ref, w1_ref, w2_ref, pb_ref,
    xs_ref, fs_ref, ps_ref, feat_ref, stat_ref,
):
    planes, rows, chans, width = own_ref.shape
    half = planes // 2
    halo = 2
    both = 2 * rows
    lead = rows - 1
    core, over, first_plane, all_planes, fracs = place_of(depth, planes)
    left = slice(0, width)
    right = slice(width, 2 * width)

    def fill(c, flip):
        blocks = (own_ref, sib_ref) if c == 0 else (sib_ref, own_ref)
        base = halo * (1 - c)
        mine = slice(base, base + planes)
        zs = slice(0, halo) if c == 0 else slice(planes, planes + halo)
        for cols, start in ((left, -1), (right, lead - 1)):
            for slot in range(rows + 2):
                row = start + slot
                if row < 0:
                    xs_ref[:, slot, :, cols] = jnp.zeros((planes + halo, chans, width), BF16)
                    continue
                row = both - 1 - row if flip else row
                xs_ref[mine, slot, :, cols] = blocks[row // rows][:, row % rows]
                xs_ref[zs, slot, :, cols] = zh_ref[:, row]
        mine_p = slice(half * c, half * c + half)
        priors = (op_ref, sp_ref) if c == 0 else (sp_ref, op_ref)
        for k in range(2):
            ps_ref[k] = priors[1 - k if flip else k][mine_p]

    for c in range(2):
        for flip in (False, True):
            pl.when(jnp.logical_and(core == c, over == flip))(functools.partial(fill, c, flip))

    deep = (half + 2) * 3 * chans
    w1 = w1_ref[...]
    fs_ref[:, 0, :, left] = jnp.zeros((half + 2, chans, width), BF16)
    for g in range(0, half + 2, half):
        for i in range(rows):
            def store(j, a, b, i=i):
                fs_ref[j, i + 1, :, left] = a
                fs_ref[j, i + 1, :, right] = b
                if i == lead - 1:
                    fs_ref[j, 0, :, right] = a

            x = xs_ref[g : g + half + 2, i : i + 3].reshape(deep, 2 * width)
            first_layer(w1, x, half, chans, first_plane, g, all_planes, store)

    w2 = w2_ref[...]
    pb = pb_ref[...]
    for i in range(lead):
        x = fs_ref[:, i : i + 3].reshape(deep, 2 * width)
        second_layer(w2, x, pb, ps_ref, fracs, (i, i + lead), over, feat_ref, stat_ref)


def outer_kernel(
    depth, side_ref, corner_ref, xs_ref, fs_ref, ps_ref, fi_ref, ti_ref, w1_ref, w2_ref, pb_ref,
    keep_ref, stat_ref, send_ref, halo_ref, late_ref, feat_ref, all_ref,
):
    planes, halo, chans, width = side_ref.shape
    half = planes // 2
    rows = keep_ref.shape[0]
    core, over, first_plane, all_planes, fracs = place_of(depth, planes)
    right = slice(width, 2 * width)

    def fill(c):
        base = halo * (1 - c)
        zs = 0 if c == 0 else planes
        for k in range(halo):
            at = jnp.where(over, halo - 1 - k, k)
            for p in range(planes):
                halo_ref[base + p, k] = side_ref[p, at]
            for p in range(halo):
                halo_ref[zs + p, k] = corner_ref[p, at]

    for c in range(2):
        pl.when(core == c)(functools.partial(fill, c))

    def pair(parts):
        return jnp.concatenate(
            [jnp.concatenate(p, axis=1).reshape(-1, width) for p in parts], axis=1
        )

    w1 = w1_ref[...]
    for g in range(0, half + 2, half):
        span = slice(g, g + half + 2)
        x = pair(
            [
                [xs_ref[span, rows:, :, right], halo_ref[span, :1]],
                [xs_ref[span, rows + 1 :, :, right], halo_ref[span]],
            ]
        )

        def store(j, a, b):
            late_ref[j, 0] = a
            late_ref[j, 1] = b

        first_layer(w1, x, half, chans, first_plane, g, all_planes, store)

    feat_ref[...] = fi_ref[...]
    all_ref[...] = ti_ref[...]
    x = pair(
        [
            [fs_ref[:, rows - 1 :, :, right], late_ref[:, :1]],
            [fs_ref[:, rows:, :, right], late_ref[...]],
        ]
    )
    two_rows = (2 * rows - 2, 2 * rows - 1)
    second_layer(w2_ref[...], x, pb_ref[...], ps_ref, fracs, two_rows, over, feat_ref, all_ref)
    kept = jnp.where(over, 1 - core, core)
    keep_ref[...] = feat_ref[kept]
    stat_ref[...] = all_ref[kept]
    given = 1 - kept
    feats = [feat_ref[given, i] for i in range(rows)]
    store_parcel(send_ref, feats, *[all_ref[given, k] for k in range(3)])


def merge(one, two, rows):
    (feat_a, stats_a), (feat_b, stats_b) = one, two
    peak = jnp.maximum(stats_a[0], stats_b[0])
    wa = jnp.exp(stats_a[0] - peak)
    wb = jnp.exp(stats_b[0] - peak)
    total = wa * stats_a[1] + wb * stats_b[1]
    depth = wa * stats_a[2] + wb * stats_b[2]
    feats = [
        wa[i : i + 1] * feat_a(i) + wb[i : i + 1] * feat_b(i) for i in range(rows)
    ]
    return feats, peak, total, depth


def parcel(ref, rows):
    chans = ref.shape[0] // rows - 6
    return (lambda i: ref[i * chans : (i + 1) * chans].astype(F32)), load_stats(ref, rows)


def first_merge_kernel(keep_ref, stat_ref, got_ref, out_ref):
    rows = keep_ref.shape[0]
    mine = (lambda i: keep_ref[i]), tuple(stat_ref[k] for k in range(3))
    store_parcel(out_ref, *merge(mine, parcel(got_ref, rows), rows))


def merge_kernel(step, rows, own_ref, got_ref, out_ref):
    low = (lax.axis_index("depth") // step) % 2 == 0

    def go(a_ref, b_ref):
        store_parcel(out_ref, *merge(parcel(a_ref, rows), parcel(b_ref, rows), rows))

    pl.when(low)(lambda: go(own_ref, got_ref))
    pl.when(jnp.logical_not(low))(lambda: go(got_ref, own_ref))


def last_merge_kernel(step, own_ref, got_ref, joined_ref, depth_ref):
    rows = joined_ref.shape[0]
    low = (lax.axis_index("depth") // step) % 2 == 0

    def go(a_ref, b_ref):
        feats, _, total, depth = merge(parcel(a_ref, rows), parcel(b_ref, rows), rows)
        inverse = 1.0 / total
        for i in range(rows):
            joined_ref[i] = feats[i] * inverse[i : i + 1]
        depth_ref[...] = depth * inverse

    pl.when(low)(lambda: go(own_ref, got_ref))
    pl.when(jnp.logical_not(low))(lambda: go(got_ref, own_ref))


def call(kernel, outs, *args, scratch=(), flops=0, nbytes=0, room=4):
    return pl.pallas_call(
        kernel,
        out_shape=[jax.ShapeDtypeStruct(s, t) for s, t in outs],
        in_specs=[VMEM] * len(args),
        out_specs=[VMEM] * len(outs),
        scratch_shapes=list(scratch),
        cost_estimate=pl.CostEstimate(flops=flops, bytes_accessed=nbytes, transcendentals=0),
        compiler_params=pltpu.CompilerParams(vmem_limit_bytes=room * 2**20),
    )(*args)


def body(volume, prior, first_kernel, second_kernel, projection):
    planes, rows, chans, width = volume.shape
    depth, rows_axis = lax.axis_size("depth"), lax.axis_size("rows")
    shape = (depth, rows_axis)
    half = planes // 2
    halo = 2
    taps = first_kernel.shape[0]
    columns = rows_axis // 2
    assert half == halo and columns == 2 and rows_axis == 4 and depth & (depth - 1) == 0

    def move(value, target):
        return exchange(value, shape, target)

    weight_shape = (taps * half * chans, (half + 2) * taps * chans)
    w1, w2, pb = call(
        prepare_kernel,
        [(weight_shape, BF16), (weight_shape, BF16), ((chans, width), F32)],
        first_kernel, second_kernel, projection[None, :],
        flops=10**8, nbytes=10**6,
    )

    core = lax.axis_index("rows") % 2
    col = lax.axis_index("rows") // 2
    lower = core == 0
    beside = move(volume, lambda d, r: (d, r ^ 1))
    prior_beside = move(prior, lambda d, r: (d, r ^ 1))
    beside, prior_beside = lax.optimization_barrier((beside, prior_beside))

    high = slice(0, halo)
    low = slice(rows - halo, rows)

    def parts(block):
        picked = jnp.where(lower, block[:half], block[half:])
        return picked, block[:, high], block[:, low]

    edge_shape = (planes, halo, chans, width)
    own_pick, own_high, own_low = call(
        cut_kernel,
        [((half, rows, chans, width), BF16), (edge_shape, BF16), (edge_shape, BF16)],
        volume,
    )
    sib_pick, sib_high, sib_low = parts(beside)
    edge = jnp.where(
        lower,
        jnp.concatenate([own_pick, sib_pick], axis=1),
        jnp.concatenate([sib_pick, own_pick], axis=1),
    )
    top_high = jnp.where(lower, own_high, sib_high)
    bottom_low = jnp.where(lower, sib_low, own_low)
    up = lambda d, r: (d + 1, r ^ 1) if r % 2 else (d - 1, r ^ 1)
    zh = move(edge, up)
    pay = jnp.where(col == 0, bottom_low, top_high)
    corner = jnp.where(lower, pay[:half], pay[half:])
    side = move(pay, lambda d, r: (d, r ^ 2))
    corner = move(corner, lambda d, r: (up(d, r)[0], r ^ 3))

    parcel_shape = (rows * (chans + 6), width)
    stats_shape = (3, rows, width)
    inside = call(
        functools.partial(inner_kernel, depth),
        [
            ((planes + halo, rows + 2, chans, 2 * width), BF16),
            ((half + 2, rows + 1, chans, 2 * width), BF16),
            ((2, half, rows, width), F32),
            ((2, rows, chans, width), F32),
            ((2,) + stats_shape, F32),
        ],
        volume, beside, zh, prior, prior_beside, w1, w2, pb,
        flops=5 * 10**8, nbytes=10**6, room=6,
    )
    keep, stat, send = call(
        functools.partial(outer_kernel, depth),
        [((rows, chans, width), F32), (stats_shape, F32), (parcel_shape, BF16)],
        side, corner, *inside, w1, w2, pb,
        scratch=[
            pltpu.VMEM((planes + halo, halo, chans, width), BF16),
            pltpu.VMEM((half + 2, halo, chans, width), BF16),
            pltpu.VMEM((2, rows, chans, width), F32),
            pltpu.VMEM((2,) + stats_shape, F32),
        ],
        flops=10**8, nbytes=10**6, room=6,
    )
    got = move(send, lambda d, r: (d, r ^ 1))
    (sums,) = call(first_merge_kernel, [(parcel_shape, BF16)], keep, stat, got)
    step = 1
    while step < depth:
        got = move(sums, lambda d, r: (d ^ step, r))
        if 2 * step < depth:
            (sums,) = call(functools.partial(merge_kernel, step, rows), [(parcel_shape, BF16)], sums, got)
        else:
            joined, depth_estimate = call(
                functools.partial(last_merge_kernel, step),
                [((rows, chans, width), F32), ((rows, width), F32)],
                sums, got,
            )
        step *= 2
    return joined, depth_estimate


def solution(mesh):
    placed = (
        P(("tiles", "depth"), "rows", None, None),
        P(("tiles", "depth"), "rows", None),
        P(),
        P(),
        P(),
    )
    return jax.shard_map(
        body,
        mesh=mesh,
        in_specs=placed,
        out_specs=(P(("tiles", "rows"), None, None), P(("tiles", "rows"), None)),
        check_vma=False,
    )
```

```python
import functools

import jax
import jax.numpy as jnp
from jax import lax
from jax.experimental import pallas as pl
from jax.experimental.pallas import tpu as pltpu
from jax.sharding import PartitionSpec as P


F32 = jnp.float32
BF16 = jnp.bfloat16
AXES = ("depth", "rows")
VMEM = pl.BlockSpec(memory_space=pltpu.VMEM)


def exchange(value, shape, target):
    depth, rows = shape
    pairs = []
    for d in range(depth):
        for r in range(rows):
            to_d, to_r = target(d, r)
            if 0 <= to_d < depth and 0 <= to_r < rows:
                pairs.append((d * rows + r, to_d * rows + to_r))
    return lax.ppermute(value, AXES, pairs)


def prepare_kernel(k1_ref, k2_ref, proj_ref, w1_ref, w2_ref, pb_ref):
    taps = k1_ref.shape[0]
    chans = k1_ref.shape[3]
    span = taps * chans
    turned_over = (lax.axis_index("rows") >> 1) == 1
    row_tap = [jnp.where(turned_over, taps - 1 - b, b) for b in range(taps)]
    for k_ref, w_ref in ((k1_ref, w1_ref), (k2_ref, w2_ref)):
        made = w_ref.shape[0] // (taps * chans)
        for e in range(taps):
            flat = jnp.concatenate(
                [k_ref[a, row_tap[b], e].astype(F32) for a in range(taps) for b in range(taps)]
                + [jnp.zeros(((made - 1) * span, chans), F32)],
                axis=0,
            )
            turned = flat.T
            for p in range(made):
                moved = turned if p == 0 else pltpu.roll(turned, p * span, 1)
                at = (e * made + p) * chans
                w_ref[at : at + chans, :] = moved.astype(BF16)
    lanes = pb_ref.shape[1]
    pb_ref[...] = jnp.broadcast_to(proj_ref[...], (lanes, chans)).T


def cut_kernel(block_ref, pick_ref, high_ref, low_ref):
    half, halo = pick_ref.shape[0], high_ref.shape[1]
    rows = block_ref.shape[1]
    core = (lax.axis_index("rows") & 1)
    pick_ref[...] = block_ref[pl.ds(core * half, half)]
    high_ref[...] = block_ref[:, :halo]
    low_ref[...] = block_ref[:, rows - halo :]


def shifted_sum(y, group):
    width = y.shape[1] // 2
    lane = lax.broadcasted_iota(jnp.int32, (1, width), 1)
    parts = []
    for s in range(2):
        cols = slice(s * width, (s + 1) * width)
        before = pltpu.roll(y[:group, cols], 1, 1)
        here = y[group : 2 * group, cols]
        after = pltpu.roll(y[2 * group :, cols], width - 1, 1)
        parts.append(
            here + jnp.where(lane == 0, 0.0, before) + jnp.where(lane == width - 1, 0.0, after)
        )
    return parts


def pieces(value, count):
    out = []
    for _ in range(count - 1):
        top = value.astype(BF16).astype(F32)
        out.append(top)
        value = value - top
    return out + [value]


def stat_pieces(peak, total, depth):
    return pieces(peak * 0.5, 3) + pieces(total, 2) + [depth]


def store_parcel(ref, feats, peak, total, depth):
    chans = feats[0].shape[0]
    for i, feat in enumerate(feats):
        ref[i * chans : (i + 1) * chans] = feat.astype(BF16)
    flat = stat_pieces(peak, total, depth)
    ref[len(feats) * chans :] = jnp.concatenate(flat, axis=0).astype(BF16)


def load_stats(ref, rows):
    flat = ref[ref.shape[0] - 6 * rows :].astype(F32)
    flat = [flat[k * rows : (k + 1) * rows] for k in range(6)]
    return ((flat[0] + flat[1]) + flat[2]) * 2.0, flat[3] + flat[4], flat[5]


def first_layer(w, x, half, chans, first_plane, g, all_planes, store):
    lo, hi = shifted_sum(jnp.dot(w, x, preferred_element_type=F32), half * chans)
    for p in range(half):
        part = slice(p * chans, (p + 1) * chans)
        a, b = jnp.maximum(lo[part], 0.0), jnp.maximum(hi[part], 0.0)
        if g + p == 0 or g + p == half + 1:
            plane = first_plane + g + p
            outside = jnp.logical_or(plane < 0, plane >= all_planes)
            a = jnp.where(outside, 0.0, a)
            b = jnp.where(outside, 0.0, b)
        store(g + p, a.astype(BF16), b.astype(BF16))


def second_layer(w, x, pb, ps_ref, fracs, two_rows, over, feat_ref, stat_ref):
    chans = feat_ref.shape[2]
    rows = feat_ref.shape[1]
    half = len(fracs)
    y = jnp.dot(w, x, preferred_element_type=F32)
    for row, side in zip(two_rows, shifted_sum(y, half * chans)):
        far = row // rows
        at = jnp.where(over, rows - 1 - row % rows, row % rows)
        side = jnp.maximum(side, 0.0).astype(BF16).astype(F32)
        feats = [side[p * chans : (p + 1) * chans] for p in range(half)]
        scores = [
            jnp.sum(feats[p] * pb, axis=0, keepdims=True) + ps_ref[far, p, pl.ds(at, 1), :]
            for p in range(half)
        ]
        peak = functools.reduce(jnp.maximum, scores)
        weights = [jnp.exp(s_ - peak) for s_ in scores]
        total = functools.reduce(jnp.add, weights)
        depth_sum = functools.reduce(jnp.add, [w_ * f for w_, f in zip(weights, fracs)])
        feat_ref[far, at] = functools.reduce(jnp.add, [w_ * f for w_, f in zip(weights, feats)])
        for k, value in enumerate((peak, total, depth_sum)):
            stat_ref[far, k, pl.ds(at, 1), :] = value


def place_of(depth, planes):
    half = planes // 2
    core = (lax.axis_index("rows") & 1)
    over = (lax.axis_index("rows") >> 1) == 1
    first_plane = lax.axis_index("depth") * planes + core * half - 1
    all_planes = depth * planes
    fracs = [((first_plane + 1 + p).astype(F32) + 0.5) / all_planes for p in range(half)]
    return core, over, first_plane, all_planes, fracs


def inner_kernel(
    depth, own_ref, sib_ref, zh_ref, op_ref, sp_ref, w1_ref, w2_ref, pb_ref,
    xs_ref, fs_ref, ps_ref, feat_ref, stat_ref,
):
    planes, rows, chans, width = own_ref.shape
    half = planes // 2
    halo = 2
    both = 2 * rows
    lead = rows - 1
    core, over, first_plane, all_planes, fracs = place_of(depth, planes)
    left = slice(0, width)
    right = slice(width, 2 * width)

    def fill(c, flip):
        blocks = (own_ref, sib_ref) if c == 0 else (sib_ref, own_ref)
        base = halo * (1 - c)
        mine = slice(base, base + planes)
        zs = slice(0, halo) if c == 0 else slice(planes, planes + halo)
        outside = lax.axis_index("depth") == (0 if c == 0 else depth - 1)
        zero_planes = jnp.zeros((halo, chans, width), BF16)
        for cols, start in ((left, -1), (right, lead - 1)):
            for slot in range(rows + 2):
                row = start + slot
                if row < 0:
                    xs_ref[:, slot, :, cols] = jnp.zeros((planes + halo, chans, width), BF16)
                    continue
                row = both - 1 - row if flip else row
                xs_ref[mine, slot, :, cols] = blocks[row // rows][:, row % rows]
                xs_ref[zs, slot, :, cols] = jnp.where(outside, zero_planes, zh_ref[:, row])
        mine_p = slice(half * c, half * c + half)
        priors = (op_ref, sp_ref) if c == 0 else (sp_ref, op_ref)
        for k in range(2):
            ps_ref[k] = priors[1 - k if flip else k][mine_p]

    for c in range(2):
        for flip in (False, True):
            pl.when(jnp.logical_and(core == c, over == flip))(functools.partial(fill, c, flip))

    deep = (half + 2) * 3 * chans
    w1 = w1_ref[...]
    fs_ref[:, 0, :, left] = jnp.zeros((half + 2, chans, width), BF16)
    for g in range(0, half + 2, half):
        for i in range(rows):
            def store(j, a, b, i=i):
                fs_ref[j, i + 1, :, left] = a
                fs_ref[j, i + 1, :, right] = b
                if i == lead - 1:
                    fs_ref[j, 0, :, right] = a

            x = xs_ref[g : g + half + 2, i : i + 3].reshape(deep, 2 * width)
            first_layer(w1, x, half, chans, first_plane, g, all_planes, store)

    w2 = w2_ref[...]
    pb = pb_ref[...]
    for i in range(lead):
        x = fs_ref[:, i : i + 3].reshape(deep, 2 * width)
        second_layer(w2, x, pb, ps_ref, fracs, (i, i + lead), over, feat_ref, stat_ref)


def outer_kernel(
    depth, side_ref, corner_ref, xs_ref, fs_ref, ps_ref, fi_ref, ti_ref, w1_ref, w2_ref, pb_ref,
    keep_ref, stat_ref, send_ref, halo_ref, late_ref, feat_ref, all_ref,
):
    planes, halo, chans, width = side_ref.shape
    half = planes // 2
    rows = keep_ref.shape[0]
    core, over, first_plane, all_planes, fracs = place_of(depth, planes)
    right = slice(width, 2 * width)

    def fill(c):
        base = halo * (1 - c)
        zs = 0 if c == 0 else planes
        outside = lax.axis_index("depth") == (0 if c == 0 else depth - 1)
        for k in range(halo):
            at = jnp.where(over, halo - 1 - k, k)
            for p in range(planes):
                halo_ref[base + p, k] = side_ref[p, at]
            for p in range(halo):
                got = corner_ref[p, at]
                halo_ref[zs + p, k] = jnp.where(outside, jnp.zeros_like(got), got)

    for c in range(2):
        pl.when(core == c)(functools.partial(fill, c))

    def pair(parts):
        return jnp.concatenate(
            [jnp.concatenate(p, axis=1).reshape(-1, width) for p in parts], axis=1
        )

    w1 = w1_ref[...]
    for g in range(0, half + 2, half):
        span = slice(g, g + half + 2)
        x = pair(
            [
                [xs_ref[span, rows:, :, right], halo_ref[span, :1]],
                [xs_ref[span, rows + 1 :, :, right], halo_ref[span]],
            ]
        )

        def store(j, a, b):
            late_ref[j, 0] = a
            late_ref[j, 1] = b

        first_layer(w1, x, half, chans, first_plane, g, all_planes, store)

    feat_ref[...] = fi_ref[...]
    all_ref[...] = ti_ref[...]
    x = pair(
        [
            [fs_ref[:, rows - 1 :, :, right], late_ref[:, :1]],
            [fs_ref[:, rows:, :, right], late_ref[...]],
        ]
    )
    two_rows = (2 * rows - 2, 2 * rows - 1)
    second_layer(w2_ref[...], x, pb_ref[...], ps_ref, fracs, two_rows, over, feat_ref, all_ref)
    kept = jnp.where(over, 1 - core, core)
    keep_ref[...] = feat_ref[kept]
    stat_ref[...] = all_ref[kept]
    given = 1 - kept
    feats = [feat_ref[given, i] for i in range(rows)]
    store_parcel(send_ref, feats, *[all_ref[given, k] for k in range(3)])


def merge(one, two, rows):
    (feat_a, stats_a), (feat_b, stats_b) = one, two
    peak = jnp.maximum(stats_a[0], stats_b[0])
    wa = jnp.exp(stats_a[0] - peak)
    wb = jnp.exp(stats_b[0] - peak)
    total = wa * stats_a[1] + wb * stats_b[1]
    depth = wa * stats_a[2] + wb * stats_b[2]
    feats = [
        wa[i : i + 1] * feat_a(i) + wb[i : i + 1] * feat_b(i) for i in range(rows)
    ]
    return feats, peak, total, depth


def parcel(ref, rows):
    chans = ref.shape[0] // rows - 6
    return (lambda i: ref[i * chans : (i + 1) * chans].astype(F32)), load_stats(ref, rows)


def first_merge_kernel(keep_ref, stat_ref, got_ref, out_ref):
    rows = keep_ref.shape[0]
    mine = (lambda i: keep_ref[i]), tuple(stat_ref[k] for k in range(3))
    store_parcel(out_ref, *merge(mine, parcel(got_ref, rows), rows))


def is_low(steps):
    step = jnp.where((lax.axis_index("rows") & 1) == 0, steps[0], steps[1])
    return (lax.axis_index("depth") & step) == 0


def merge_kernel(steps, rows, own_ref, got_ref, out_ref):
    low = is_low(steps)

    def go(a_ref, b_ref):
        store_parcel(out_ref, *merge(parcel(a_ref, rows), parcel(b_ref, rows), rows))

    pl.when(low)(lambda: go(own_ref, got_ref))
    pl.when(jnp.logical_not(low))(lambda: go(got_ref, own_ref))


def last_merge_kernel(steps, own_ref, got_ref, joined_ref, depth_ref):
    rows = joined_ref.shape[0]
    low = is_low(steps)

    def go(a_ref, b_ref):
        feats, _, total, depth = merge(parcel(a_ref, rows), parcel(b_ref, rows), rows)
        inverse = 1.0 / total
        for i in range(rows):
            joined_ref[i] = feats[i] * inverse[i : i + 1]
        depth_ref[...] = depth * inverse

    pl.when(low)(lambda: go(own_ref, got_ref))
    pl.when(jnp.logical_not(low))(lambda: go(got_ref, own_ref))


def call(kernel, outs, *args, scratch=(), flops=0, nbytes=0, room=4):
    return pl.pallas_call(
        kernel,
        out_shape=[jax.ShapeDtypeStruct(s, t) for s, t in outs],
        in_specs=[VMEM] * len(args),
        out_specs=[VMEM] * len(outs),
        scratch_shapes=list(scratch),
        cost_estimate=pl.CostEstimate(flops=flops, bytes_accessed=nbytes, transcendentals=0),
        compiler_params=pltpu.CompilerParams(vmem_limit_bytes=room * 2**20),
    )(*args)


def body(volume, prior, first_kernel, second_kernel, projection):
    planes, rows, chans, width = volume.shape
    depth, rows_axis = lax.axis_size("depth"), lax.axis_size("rows")
    shape = (depth, rows_axis)
    half = planes // 2
    halo = 2
    taps = first_kernel.shape[0]
    columns = rows_axis // 2
    assert half == halo and columns == 2 and rows_axis == 4 and depth & (depth - 1) == 0

    def move(value, target):
        return exchange(value, shape, target)

    weight_shape = (taps * half * chans, (half + 2) * taps * chans)
    w1, w2, pb = call(
        prepare_kernel,
        [(weight_shape, BF16), (weight_shape, BF16), ((chans, width), F32)],
        first_kernel, second_kernel, projection[None, :],
        flops=10**8, nbytes=10**6,
    )

    core = (lax.axis_index("rows") & 1)
    col = (lax.axis_index("rows") >> 1)
    lower = core == 0
    beside = move(volume, lambda d, r: (d, r ^ 1))
    prior_beside = move(prior, lambda d, r: (d, r ^ 1))
    beside, prior_beside = lax.optimization_barrier((beside, prior_beside))

    high = slice(0, halo)
    low = slice(rows - halo, rows)

    def parts(block):
        picked = jnp.where(lower, block[:half], block[half:])
        return picked, block[:, high], block[:, low]

    edge_shape = (planes, halo, chans, width)
    own_pick, own_high, own_low = call(
        cut_kernel,
        [((half, rows, chans, width), BF16), (edge_shape, BF16), (edge_shape, BF16)],
        volume,
    )
    sib_pick, sib_high, sib_low = parts(beside)
    edge = jnp.where(
        lower,
        jnp.concatenate([own_pick, sib_pick], axis=1),
        jnp.concatenate([sib_pick, own_pick], axis=1),
    )
    top_high = jnp.where(lower, own_high, sib_high)
    bottom_low = jnp.where(lower, sib_low, own_low)

    def up(d, r):
        to = d + 1 if r % 2 else d - 1
        return (to, r ^ 1) if 0 <= to < depth else (d, r ^ 2)

    def up_across(d, r):
        to = d + 1 if r % 2 else d - 1
        return (to, r ^ 3) if 0 <= to < depth else (d, r ^ 2)

    zh = move(edge, up)
    pay = jnp.where(col == 0, bottom_low, top_high)
    corner = jnp.where(lower, pay[:half], pay[half:])
    side = move(pay, lambda d, r: (d, r ^ 2))
    corner = move(corner, up_across)

    parcel_shape = (rows * (chans + 6), width)
    stats_shape = (3, rows, width)
    inside = call(
        functools.partial(inner_kernel, depth),
        [
            ((planes + halo, rows + 2, chans, 2 * width), BF16),
            ((half + 2, rows + 1, chans, 2 * width), BF16),
            ((2, half, rows, width), F32),
            ((2, rows, chans, width), F32),
            ((2,) + stats_shape, F32),
        ],
        volume, beside, zh, prior, prior_beside, w1, w2, pb,
        flops=5 * 10**8, nbytes=10**6, room=6,
    )
    keep, stat, send = call(
        functools.partial(outer_kernel, depth),
        [((rows, chans, width), F32), (stats_shape, F32), (parcel_shape, BF16)],
        side, corner, *inside, w1, w2, pb,
        scratch=[
            pltpu.VMEM((planes + halo, halo, chans, width), BF16),
            pltpu.VMEM((half + 2, halo, chans, width), BF16),
            pltpu.VMEM((2, rows, chans, width), F32),
            pltpu.VMEM((2,) + stats_shape, F32),
        ],
        flops=10**8, nbytes=10**6, room=6,
    )
    got = move(send, lambda d, r: (d, r ^ 1))
    (sums,) = call(first_merge_kernel, [(parcel_shape, BF16)], keep, stat, got)
    order = [1 << k for k in range(depth.bit_length() - 1)]
    for k, steps in enumerate(zip(order[::-1], order)):
        got = move(sums, lambda d, r: (d ^ steps[r & 1], r))
        if k + 1 < len(order):
            (sums,) = call(
                functools.partial(merge_kernel, steps, rows), [(parcel_shape, BF16)], sums, got
            )
        else:
            joined, depth_estimate = call(
                functools.partial(last_merge_kernel, steps),
                [((rows, chans, width), F32), ((rows, width), F32)],
                sums, got,
            )
    return joined, depth_estimate


def solution(mesh):
    placed = (
        P(("tiles", "depth"), "rows", None, None),
        P(("tiles", "depth"), "rows", None),
        P(),
        P(),
        P(),
    )
    return jax.shard_map(
        body,
        mesh=mesh,
        in_specs=placed,
        out_specs=(P(("tiles", "rows"), None, None), P(("tiles", "rows"), None)),
        check_vma=False,
    )
```

```python
import functools

import jax
import jax.numpy as jnp
from jax import lax
from jax.experimental import pallas as pl
from jax.experimental.pallas import tpu as pltpu
from jax.sharding import PartitionSpec as P


F32 = jnp.float32
BF16 = jnp.bfloat16
AXES = ("depth", "rows")
STATS = 6
VMEM = pl.BlockSpec(memory_space=pltpu.VMEM)


def exchange(value, shape, target):
    depth, rows = shape
    pairs = []
    for d in range(depth):
        for r in range(rows):
            to_d, to_r = target(d, r)
            if 0 <= to_d < depth and 0 <= to_r < rows:
                pairs.append((d * rows + r, to_d * rows + to_r))
    return lax.ppermute(value, AXES, pairs)


def prepare_kernel(k1_ref, k2_ref, proj_ref, w1_ref, w2_ref, pb_ref):
    taps = k1_ref.shape[0]
    chans = k1_ref.shape[3]
    span = taps * chans
    turned_over = (lax.axis_index("rows") >> 1) == 1
    row_tap = [jnp.where(turned_over, taps - 1 - b, b) for b in range(taps)]
    for k_ref, w_ref in ((k1_ref, w1_ref), (k2_ref, w2_ref)):
        made = w_ref.shape[0] // (taps * chans)
        for e in range(taps):
            flat = jnp.concatenate(
                [k_ref[a, row_tap[b], e].astype(F32) for a in range(taps) for b in range(taps)]
                + [jnp.zeros(((made - 1) * span, chans), F32)],
                axis=0,
            )
            turned = flat.T
            for p in range(made):
                moved = turned if p == 0 else pltpu.roll(turned, p * span, 1)
                at = (e * made + p) * chans
                w_ref[at : at + chans, :] = moved.astype(BF16)
    lanes = pb_ref.shape[1]
    pb_ref[...] = jnp.broadcast_to(proj_ref[...], (lanes, chans)).T


def cut_kernel(block_ref, pick_ref, high_ref, low_ref):
    half, halo = pick_ref.shape[0], high_ref.shape[1]
    rows = block_ref.shape[1]
    core = (lax.axis_index("rows") & 1)
    pick_ref[...] = block_ref[pl.ds(core * half, half)]
    high_ref[...] = block_ref[:, :halo]
    low_ref[...] = block_ref[:, rows - halo :]


def shifted_sum(y, group):
    width = y.shape[1] // 2
    lane = lax.broadcasted_iota(jnp.int32, (1, width), 1)
    parts = []
    for s in range(2):
        cols = slice(s * width, (s + 1) * width)
        before = pltpu.roll(y[:group, cols], 1, 1)
        here = y[group : 2 * group, cols]
        after = pltpu.roll(y[2 * group :, cols], width - 1, 1)
        parts.append(
            here + jnp.where(lane == 0, 0.0, before) + jnp.where(lane == width - 1, 0.0, after)
        )
    return parts


def pieces(value, count):
    out = []
    for _ in range(count - 1):
        top = value.astype(BF16).astype(F32)
        out.append(top)
        value = value - top
    return out + [value]


def stat_pieces(peak, total, depth):
    return pieces(peak * 0.5, 3) + pieces(total, 2) + [depth]


def store_parcel(ref, feats, peak, total, depth):
    chans = feats[0].shape[0]
    for i, feat in enumerate(feats):
        ref[i * chans : (i + 1) * chans] = feat.astype(BF16)
    flat = stat_pieces(peak, total, depth)
    ref[len(feats) * chans :] = jnp.concatenate(flat, axis=0).astype(BF16)


def load_stats(ref, rows):
    flat = ref[ref.shape[0] - STATS * rows :].astype(F32)
    flat = [flat[k * rows : (k + 1) * rows] for k in range(STATS)]
    return ((flat[0] + flat[1]) + flat[2]) * 2.0, flat[3] + flat[4], flat[5]


def first_layer(w, x, half, chans, outside, store):
    lo, hi = shifted_sum(jnp.dot(w, x, preferred_element_type=F32), half * chans)
    for p in range(half):
        part = slice(p * chans, (p + 1) * chans)
        a, b = jnp.maximum(lo[part], 0.0), jnp.maximum(hi[part], 0.0)
        if outside is not None:
            a = jnp.where(outside[p], 0.0, a)
            b = jnp.where(outside[p], 0.0, b)
        store(p, a.astype(BF16), b.astype(BF16))


def second_layer(w, x, pb, ps_ref, fracs, two_rows, over, feat_ref, stat_ref):
    chans = feat_ref.shape[2]
    rows = feat_ref.shape[1]
    half = len(fracs)
    y = jnp.dot(w, x, preferred_element_type=F32)
    for row, side in zip(two_rows, shifted_sum(y, half * chans)):
        far = row // rows
        at = jnp.where(over, rows - 1 - row % rows, row % rows)
        side = jnp.maximum(side, 0.0).astype(BF16).astype(F32)
        feats = [side[p * chans : (p + 1) * chans] for p in range(half)]
        scores = [
            jnp.sum(feats[p] * pb, axis=0, keepdims=True) + ps_ref[far, p, pl.ds(at, 1), :]
            for p in range(half)
        ]
        peak = functools.reduce(jnp.maximum, scores)
        weights = [jnp.exp(s_ - peak) for s_ in scores]
        total = functools.reduce(jnp.add, weights)
        depth_sum = functools.reduce(jnp.add, [w_ * f for w_, f in zip(weights, fracs)])
        feat_ref[far, at] = functools.reduce(jnp.add, [w_ * f for w_, f in zip(weights, feats)])
        for k, value in enumerate((peak, total, depth_sum)):
            stat_ref[far, k, pl.ds(at, 1), :] = value


def place_of(depth, planes):
    half = planes // 2
    d = lax.axis_index("depth")
    core = lax.axis_index("rows") & 1
    over = (lax.axis_index("rows") >> 1) == 1
    fracs = [
        ((d * planes + core * half + p).astype(F32) + 0.5) / (depth * planes) for p in range(half)
    ]
    first, last = d == 0, d == depth - 1
    outside = [jnp.logical_and(core == 0, first)] + [False] * (half - 2)
    outside = outside + [jnp.logical_and(core == 1, last)]
    return core, over, fracs, outside


def by_place(core, over, fill):
    for c in range(2):
        for flip in (False, True):
            pl.when(jnp.logical_and(core == c, over == flip))(functools.partial(fill, c, flip))


def fill_rows(ref, to, source, planes, rows, flip):
    chans, width = ref.shape[2], ref.shape[3] // 2
    for cols, start in ((slice(0, width), -1), (slice(width, 2 * width), rows - 2)):
        for slot in range(rows + 2):
            row = start + slot
            if row < 0:
                ref[to, slot, :, cols] = jnp.zeros((planes, chans, width), BF16)
            else:
                ref[to, slot, :, cols] = source(2 * rows - 1 - row if flip else row)


def first_rows(w, x_ref, half, rows, outside, fs_ref, base):
    chans, wide = x_ref.shape[2:]
    left, right = slice(0, wide // 2), slice(wide // 2, wide)
    for p in range(half):
        fs_ref[base + p, 0, :, left] = jnp.zeros((chans, wide // 2), BF16)
    for i in range(rows):
        def store(p, a, b, i=i):
            fs_ref[base + p, i + 1, :, left] = a
            fs_ref[base + p, i + 1, :, right] = b
            if i == rows - 2:
                fs_ref[base + p, 0, :, right] = a

        x = x_ref[:, i : i + 3].reshape(-1, wide)
        first_layer(w, x, half, chans, outside, store)


def own_kernel(depth, own_ref, sib_ref, op_ref, sp_ref, w1_ref, xo_ref, fo_ref, ps_ref):
    planes, rows, _, _ = own_ref.shape
    half = planes // 2
    core, over, _, _ = place_of(depth, planes)

    def fill(c, flip):
        blocks = (own_ref, sib_ref) if c == 0 else (sib_ref, own_ref)
        fill_rows(
            xo_ref, slice(0, planes), lambda row: blocks[row // rows][:, row % rows],
            planes, rows, flip,
        )
        priors = (op_ref, sp_ref) if c == 0 else (sp_ref, op_ref)
        for k in range(2):
            ps_ref[k] = priors[1 - k if flip else k][half * c : half * c + half]

    by_place(core, over, fill)
    first_rows(w1_ref[...], xo_ref, half, rows, None, fo_ref, 0)


def inner_kernel(
    depth, zh_ref, xo_ref, fo_ref, ps_ref, w1_ref, w2_ref, pb_ref,
    xz_ref, fs_ref, feat_ref, stat_ref,
):
    half = zh_ref.shape[0]
    planes = xo_ref.shape[0]
    rows = xo_ref.shape[1] - 2
    wide = xo_ref.shape[3]
    lead = rows - 1
    core, over, fracs, outside = place_of(depth, planes)
    ends = jnp.logical_or(outside[0], outside[-1])

    def fill(c, flip):
        theirs, mine = slice(half * c, half * c + half), slice(half * (1 - c), half * (2 - c))
        xz_ref[mine] = xo_ref[theirs]
        fs_ref[mine] = fo_ref[...]
        fill_rows(
            xz_ref, theirs,
            lambda row: jnp.where(ends, jnp.zeros_like(zh_ref[:, row]), zh_ref[:, row]),
            half, rows, flip,
        )

    by_place(core, over, fill)
    first_rows(w1_ref[...], xz_ref, half, rows, outside, fs_ref, core * half)
    w2 = w2_ref[...]
    pb = pb_ref[...]
    for i in range(lead):
        x = fs_ref[:, i : i + 3].reshape(-1, wide)
        second_layer(w2, x, pb, ps_ref, fracs, (i, i + lead), over, feat_ref, stat_ref)


def outer_kernel(
    depth, side_ref, corner_ref, xo_ref, ps_ref, xz_ref, fs_ref, fi_ref, ti_ref, w1_ref, w2_ref,
    pb_ref, keep_ref, stat_ref, send_ref, own_halo_ref, halo_ref, late_ref, feat_ref, all_ref,
):
    planes, halo, chans, width = side_ref.shape
    half = planes // 2
    rows = keep_ref.shape[0]
    core, over, fracs, outside = place_of(depth, planes)
    ends = jnp.logical_or(outside[0], outside[-1])
    right = slice(width, 2 * width)

    for k in range(halo):
        at = jnp.where(over, halo - 1 - k, k)
        for p in range(planes):
            own_halo_ref[p, k] = side_ref[p, at]
        for p in range(half):
            got = corner_ref[p, at]
            halo_ref[core * half + p, k] = jnp.where(ends, jnp.zeros_like(got), got)
            halo_ref[(1 - core) * half + p, k] = side_ref[core * half + p, at]

    def pair(parts):
        return jnp.concatenate(
            [jnp.concatenate(p, axis=1).reshape(-1, width) for p in parts], axis=1
        )

    w1 = w1_ref[...]
    for x_ref, h_ref, mask, base in (
        (xo_ref, own_halo_ref, None, (1 - core) * half),
        (xz_ref, halo_ref, outside, core * half),
    ):
        x = pair(
            [
                [x_ref[:, rows:, :, right], h_ref[:, :1]],
                [x_ref[:, rows + 1 :, :, right], h_ref[...]],
            ]
        )

        def store(p, a, b):
            late_ref[base + p, 0] = a
            late_ref[base + p, 1] = b

        first_layer(w1, x, half, chans, mask, store)

    feat_ref[...] = fi_ref[...]
    all_ref[...] = ti_ref[...]
    x = pair(
        [
            [fs_ref[:, rows - 1 :, :, right], late_ref[:, :1]],
            [fs_ref[:, rows:, :, right], late_ref[...]],
        ]
    )
    two_rows = (2 * rows - 2, 2 * rows - 1)
    second_layer(w2_ref[...], x, pb_ref[...], ps_ref, fracs, two_rows, over, feat_ref, all_ref)
    kept = jnp.where(over, 1 - core, core)
    keep_ref[...] = feat_ref[kept]
    stat_ref[...] = all_ref[kept]
    given = 1 - kept
    feats = [feat_ref[given, i] for i in range(rows)]
    store_parcel(send_ref, feats, *[all_ref[given, k] for k in range(3)])


def merge(one, two, rows):
    (feat_a, stats_a), (feat_b, stats_b) = one, two
    peak = jnp.maximum(stats_a[0], stats_b[0])
    wa = jnp.exp(stats_a[0] - peak)
    wb = jnp.exp(stats_b[0] - peak)
    total = wa * stats_a[1] + wb * stats_b[1]
    depth = wa * stats_a[2] + wb * stats_b[2]
    feats = [
        wa[i : i + 1] * feat_a(i) + wb[i : i + 1] * feat_b(i) for i in range(rows)
    ]
    return feats, peak, total, depth


def parcel(ref, rows):
    chans = ref.shape[0] // rows - STATS
    return (lambda i: ref[i * chans : (i + 1) * chans].astype(F32)), load_stats(ref, rows)


def first_merge_kernel(keep_ref, stat_ref, got_ref, out_ref):
    rows = keep_ref.shape[0]
    mine = (lambda i: keep_ref[i]), tuple(stat_ref[k] for k in range(3))
    store_parcel(out_ref, *merge(mine, parcel(got_ref, rows), rows))


def merge_group(step, refs, rows, finish):
    def go(me):
        parts = [parcel(refs[me ^ j], rows) for j in range(len(refs))]
        while True:
            merged = [merge(a, b, rows) for a, b in zip(parts[::2], parts[1::2])]
            if len(merged) == 1:
                return finish(*merged[0])
            parts = [(m[0].__getitem__, m[1:]) for m in merged]

    place = (lax.axis_index("depth") // step) & (len(refs) - 1)
    for me in range(len(refs)):
        pl.when(place == me)(functools.partial(go, me))


def merge_kernel(step, rows, *refs):
    merge_group(step, refs[:-1], rows, functools.partial(store_parcel, refs[-1]))


def last_merge_kernel(step, *refs):
    joined_ref, depth_ref = refs[-2:]
    rows = joined_ref.shape[0]

    def finish(feats, peak, total, depth):
        inverse = 1.0 / total
        for i in range(rows):
            joined_ref[i] = feats[i] * inverse[i : i + 1]
        depth_ref[...] = depth * inverse

    merge_group(step, refs[:-2], rows, finish)


def merge_rounds(depth):
    rounds = []
    step = 1
    while step < depth:
        count = 4 if step * 4 <= depth else 2
        rounds.append((step, count))
        step *= count
    return rounds


def call(kernel, outs, *args, scratch=(), flops=0, nbytes=0, room=4):
    return pl.pallas_call(
        kernel,
        out_shape=[jax.ShapeDtypeStruct(s, t) for s, t in outs],
        in_specs=[VMEM] * len(args),
        out_specs=[VMEM] * len(outs),
        scratch_shapes=list(scratch),
        cost_estimate=pl.CostEstimate(flops=flops, bytes_accessed=nbytes, transcendentals=0),
        compiler_params=pltpu.CompilerParams(vmem_limit_bytes=room * 2**20),
    )(*args)


def body(volume, prior, first_kernel, second_kernel, projection):
    planes, rows, chans, width = volume.shape
    depth, rows_axis = lax.axis_size("depth"), lax.axis_size("rows")
    shape = (depth, rows_axis)
    half = planes // 2
    halo = 2
    taps = first_kernel.shape[0]
    columns = rows_axis // 2
    assert half == halo and columns == 2 and rows_axis == 4 and depth & (depth - 1) == 0

    def move(value, target):
        return exchange(value, shape, target)

    weight_shape = (taps * half * chans, (half + 2) * taps * chans)
    w1, w2, pb = call(
        prepare_kernel,
        [(weight_shape, BF16), (weight_shape, BF16), ((chans, width), F32)],
        first_kernel, second_kernel, projection[None, :],
        flops=10**8, nbytes=10**6,
    )

    core = (lax.axis_index("rows") & 1)
    col = (lax.axis_index("rows") >> 1)
    lower = core == 0
    beside = move(volume, lambda d, r: (d, r ^ 1))
    prior_beside = move(prior, lambda d, r: (d, r ^ 1))
    beside, prior_beside = lax.optimization_barrier((beside, prior_beside))

    high = slice(0, halo)
    low = slice(rows - halo, rows)

    def parts(block):
        picked = jnp.where(lower, block[:half], block[half:])
        return picked, block[:, high], block[:, low]

    edge_shape = (planes, halo, chans, width)
    own_pick, own_high, own_low = call(
        cut_kernel,
        [((half, rows, chans, width), BF16), (edge_shape, BF16), (edge_shape, BF16)],
        volume,
    )
    sib_pick, sib_high, sib_low = parts(beside)
    edge = jnp.where(
        lower,
        jnp.concatenate([own_pick, sib_pick], axis=1),
        jnp.concatenate([sib_pick, own_pick], axis=1),
    )
    top_high = jnp.where(lower, own_high, sib_high)
    bottom_low = jnp.where(lower, sib_low, own_low)

    def up(d, r):
        to = d + 1 if r % 2 else d - 1
        return (to, r ^ 1) if 0 <= to < depth else (d, r ^ 2)

    def up_across(d, r):
        to = d + 1 if r % 2 else d - 1
        return (to, r ^ 3) if 0 <= to < depth else (d, r ^ 2)

    zh = move(edge, up)
    pay = jnp.where(col == 0, bottom_low, top_high)
    corner = jnp.where(lower, pay[:half], pay[half:])
    side = move(pay, lambda d, r: (d, r ^ 3))
    corner = move(corner, up_across)

    parcel_shape = (rows * (chans + STATS), width)
    stats_shape = (3, rows, width)
    block_shape = (planes, rows + 2, chans, 2 * width)
    xo, fo, ps = call(
        functools.partial(own_kernel, depth),
        [
            (block_shape, BF16),
            ((half, rows + 1, chans, 2 * width), BF16),
            ((2, half, rows, width), F32),
        ],
        volume, beside, prior, prior_beside, w1,
        flops=2 * 10**8, nbytes=10**6, room=6,
    )
    inside = call(
        functools.partial(inner_kernel, depth),
        [
            (block_shape, BF16),
            ((half + 2, rows + 1, chans, 2 * width), BF16),
            ((2, rows, chans, width), F32),
            ((2,) + stats_shape, F32),
        ],
        zh, xo, fo, ps, w1, w2, pb,
        flops=5 * 10**8, nbytes=10**6, room=6,
    )
    keep, stat, send = call(
        functools.partial(outer_kernel, depth),
        [((rows, chans, width), F32), (stats_shape, F32), (parcel_shape, BF16)],
        side, corner, xo, ps, *inside, w1, w2, pb,
        scratch=[
            pltpu.VMEM((planes, halo, chans, width), BF16),
            pltpu.VMEM((planes, halo, chans, width), BF16),
            pltpu.VMEM((half + 2, halo, chans, width), BF16),
            pltpu.VMEM((2, rows, chans, width), F32),
            pltpu.VMEM((2,) + stats_shape, F32),
        ],
        flops=10**8, nbytes=10**6, room=6,
    )
    got = move(send, lambda d, r: (d, r ^ 1))
    (sums,) = call(first_merge_kernel, [(parcel_shape, BF16)], keep, stat, got)
    rounds = merge_rounds(depth)
    for step, count in rounds:
        others = [move(sums, lambda d, r: (d ^ (k * step), r)) for k in range(1, count)]
        if (step, count) != rounds[-1]:
            (sums,) = call(
                functools.partial(merge_kernel, step, rows), [(parcel_shape, BF16)], sums, *others
            )
    joined, depth_estimate = call(
        functools.partial(last_merge_kernel, step),
        [((rows, chans, width), F32), ((rows, width), F32)],
        sums, *others,
    )
    return joined, depth_estimate


def solution(mesh):
    placed = (
        P(("tiles", "depth"), "rows", None, None),
        P(("tiles", "depth"), "rows", None),
        P(),
        P(),
        P(),
    )
    return jax.shard_map(
        body,
        mesh=mesh,
        in_specs=placed,
        out_specs=(P(("tiles", "rows"), None, None), P(("tiles", "rows"), None)),
        check_vma=False,
    )
```

```python
import functools

import jax
import jax.numpy as jnp
from jax import lax
from jax.experimental import pallas as pl
from jax.experimental.pallas import tpu as pltpu
from jax.sharding import PartitionSpec as P


F32 = jnp.float32
BF16 = jnp.bfloat16
AXES = ("depth", "rows")
STATS = 6
VMEM = pl.BlockSpec(memory_space=pltpu.VMEM)


def exchange(value, shape, target):
    depth, rows = shape
    pairs = []
    for d in range(depth):
        for r in range(rows):
            to_d, to_r = target(d, r)
            if 0 <= to_d < depth and 0 <= to_r < rows:
                pairs.append((d * rows + r, to_d * rows + to_r))
    return lax.ppermute(value, AXES, pairs)


def prepare_kernel(k1_ref, k2_ref, proj_ref, w1_ref, w2_ref, pb_ref):
    taps = k1_ref.shape[0]
    chans = k1_ref.shape[3]
    span = taps * chans
    turned_over = (lax.axis_index("rows") >> 1) == 1
    row_tap = [jnp.where(turned_over, taps - 1 - b, b) for b in range(taps)]
    upper = (lax.axis_index("rows") & 1) == 1
    plane_tap = [jnp.where(upper, taps - 1 - a, a) for a in range(taps)]
    for k_ref, w_ref in ((k1_ref, w1_ref), (k2_ref, w2_ref)):
        made = w_ref.shape[0] // (taps * chans)
        for e in range(taps):
            flat = jnp.concatenate(
                [k_ref[plane_tap[a], row_tap[b], e].astype(F32) for a in range(taps) for b in range(taps)]
                + [jnp.zeros(((made - 1) * span, chans), F32)],
                axis=0,
            )
            turned = flat.T
            for p in range(made):
                moved = turned if p == 0 else pltpu.roll(turned, p * span, 1)
                at = (e * made + p) * chans
                w_ref[at : at + chans, :] = moved.astype(BF16)
    lanes = pb_ref.shape[1]
    pb_ref[...] = jnp.broadcast_to(proj_ref[...], (lanes, chans)).T


def cut_kernel(block_ref, pick_ref, high_ref, low_ref):
    half, halo = pick_ref.shape[0], high_ref.shape[1]
    rows = block_ref.shape[1]
    core = (lax.axis_index("rows") & 1)
    pick_ref[...] = block_ref[pl.ds(core * half, half)]
    high_ref[...] = block_ref[:, :halo]
    low_ref[...] = block_ref[:, rows - halo :]


def shifted_sum(y, group):
    width = y.shape[1] // 2
    lane = lax.broadcasted_iota(jnp.int32, (1, width), 1)
    parts = []
    for s in range(2):
        cols = slice(s * width, (s + 1) * width)
        before = pltpu.roll(y[:group, cols], 1, 1)
        here = y[group : 2 * group, cols]
        after = pltpu.roll(y[2 * group :, cols], width - 1, 1)
        parts.append(
            here + jnp.where(lane == 0, 0.0, before) + jnp.where(lane == width - 1, 0.0, after)
        )
    return parts


def pieces(value, count):
    out = []
    for _ in range(count - 1):
        top = value.astype(BF16).astype(F32)
        out.append(top)
        value = value - top
    return out + [value]


def stat_pieces(peak, total, depth):
    return pieces(peak * 0.5, 3) + pieces(total, 2) + [depth]


def store_parcel(ref, feats, peak, total, depth):
    chans = feats[0].shape[0]
    for i, feat in enumerate(feats):
        ref[i * chans : (i + 1) * chans] = feat.astype(BF16)
    flat = stat_pieces(peak, total, depth)
    ref[len(feats) * chans :] = jnp.concatenate(flat, axis=0).astype(BF16)


def load_stats(ref, rows):
    flat = ref[ref.shape[0] - STATS * rows :].astype(F32)
    flat = [flat[k * rows : (k + 1) * rows] for k in range(STATS)]
    return ((flat[0] + flat[1]) + flat[2]) * 2.0, flat[3] + flat[4], flat[5]


def first_layer(w, x, half, chans, ends, store):
    lo, hi = shifted_sum(jnp.dot(w, x, preferred_element_type=F32), half * chans)
    for p in range(half):
        part = slice(p * chans, (p + 1) * chans)
        a, b = jnp.maximum(lo[part], 0.0), jnp.maximum(hi[part], 0.0)
        if ends is not None and p == 0:
            a = jnp.where(ends, 0.0, a)
            b = jnp.where(ends, 0.0, b)
        store(p, a.astype(BF16), b.astype(BF16))


def second_layer(w, x, pb, ps_ref, fracs, two_rows, over, put, stat_ref):
    chans = pb.shape[0]
    rows = ps_ref.shape[2]
    half = len(fracs)
    y = jnp.dot(w, x, preferred_element_type=F32)
    for row, side in zip(two_rows, shifted_sum(y, half * chans)):
        far = row // rows
        at = jnp.where(over, rows - 1 - row % rows, row % rows)
        side = jnp.maximum(side, 0.0).astype(BF16).astype(F32)
        feats = [side[p * chans : (p + 1) * chans] for p in range(half)]
        scores = [
            jnp.sum(feats[p] * pb, axis=0, keepdims=True) + ps_ref[far, p, pl.ds(at, 1), :]
            for p in range(half)
        ]
        peak = functools.reduce(jnp.maximum, scores)
        weights = [jnp.exp(s_ - peak) for s_ in scores]
        total = functools.reduce(jnp.add, weights)
        depth_sum = functools.reduce(jnp.add, [w_ * f for w_, f in zip(weights, fracs)])
        put(far, at, functools.reduce(jnp.add, [w_ * f for w_, f in zip(weights, feats)]))
        for k, value in enumerate((peak, total, depth_sum)):
            stat_ref[far, k, pl.ds(at, 1), :] = value


def place_of(depth, planes):
    half = planes // 2
    d = lax.axis_index("depth")
    core = lax.axis_index("rows") & 1
    over = (lax.axis_index("rows") >> 1) == 1
    plane = [d * planes + jnp.where(core == 1, planes - 1 - p, p) for p in range(half)]
    fracs = [(p.astype(F32) + 0.5) / (depth * planes) for p in plane]
    ends = d == jnp.where(core == 1, depth - 1, 0)
    return core, over, fracs, ends


def turned(p, planes, flag):
    return jnp.where(flag, planes - 1 - p, p)


def fill_rows(ref, p, source, rows, row_of):
    chans, width = ref.shape[2], ref.shape[3] // 2
    for cols, start in ((slice(0, width), -1), (slice(width, 2 * width), rows - 2)):
        for slot in range(rows + 2):
            row = start + slot
            if row < 0:
                ref[p, slot, :, cols] = jnp.zeros((chans, width), BF16)
            else:
                ref[p, slot, :, cols] = source(row_of(row))


def first_rows(w, x_of, half, rows, ends, fs_ref):
    chans, wide = fs_ref.shape[2:]
    left, right = slice(0, wide // 2), slice(wide // 2, wide)
    for p in range(half):
        fs_ref[p, 0, :, left] = jnp.zeros((chans, wide // 2), BF16)
    for i in range(rows):
        def store(p, a, b, i=i):
            fs_ref[p, i + 1, :, left] = a
            fs_ref[p, i + 1, :, right] = b
            if i == rows - 2:
                fs_ref[p, 0, :, right] = a

        first_layer(w, x_of(slice(i, i + 3)).reshape(-1, wide), half, chans, ends, store)


def own_kernel(depth, own_ref, sib_ref, op_ref, sp_ref, w1_ref, xo_ref, fo_ref, ps_ref):
    planes, rows, _, _ = own_ref.shape
    half = planes // 2
    core, over, _, _ = place_of(depth, planes)

    def fill(c, flip):
        blocks = (own_ref, sib_ref) if c == 0 else (sib_ref, own_ref)
        priors = (op_ref, sp_ref) if c == 0 else (sp_ref, op_ref)
        for p in range(planes):
            plane = planes - 1 - p if c else p
            fill_rows(
                xo_ref, p, lambda row: blocks[row // rows][plane, row % rows], rows,
                lambda row: 2 * rows - 1 - row if flip else row,
            )
            if p < half:
                for k in range(2):
                    ps_ref[k, p] = priors[1 - k if flip else k][plane]

    for c in range(2):
        for flip in (False, True):
            pl.when(jnp.logical_and(core == c, over == flip))(functools.partial(fill, c, flip))
    first_rows(w1_ref[...], lambda at: xo_ref[:, at], half, rows, None, fo_ref)


def inner_kernel(
    depth, zh_ref, xo_ref, fo_ref, ps_ref, w1_ref, w2_ref, pb_ref,
    xz_ref, fz_ref, feat_ref, stat_ref,
):
    half = zh_ref.shape[0]
    planes = xo_ref.shape[0]
    rows = xo_ref.shape[1] - 2
    wide = xo_ref.shape[3]
    lead = rows - 1
    core, over, fracs, ends = place_of(depth, planes)
    for p in range(half):
        plane = turned(p, half, core == 1)

        def source(row):
            got = zh_ref[plane, row]
            return jnp.where(ends, jnp.zeros_like(got), got)

        fill_rows(xz_ref, p, source, rows, lambda row: turned(row, 2 * rows, over))

    first_rows(
        w1_ref[...], lambda at: jnp.concatenate([xz_ref[:, at], xo_ref[:half, at]], axis=0),
        half, rows, ends, fz_ref,
    )

    def put(far, at, feat):
        feat_ref[far, at] = feat

    w2 = w2_ref[...]
    pb = pb_ref[...]
    for i in range(lead):
        at = slice(i, i + 3)
        x = jnp.concatenate([fz_ref[:, at], fo_ref[:, at]], axis=0).reshape(-1, wide)
        second_layer(w2, x, pb, ps_ref, fracs, (i, i + lead), over, put, stat_ref)


def outer_kernel(
    depth, side_ref, corner_ref, xo_ref, fo_ref, ps_ref, xz_ref, fz_ref, fi_ref, ti_ref, w1_ref,
    w2_ref, pb_ref, keep_ref, stat_ref, send_ref, all_ref,
):
    planes, halo, chans, width = side_ref.shape
    half = planes // 2
    rows = keep_ref.shape[0]
    core, over, fracs, ends = place_of(depth, planes)
    right = slice(width, 2 * width)
    kept = jnp.where(over, 1 - core, core)
    given = 1 - kept
    keep_ref[...] = fi_ref[kept]
    for i in range(rows):
        send_ref[i * chans : (i + 1) * chans] = fi_ref[given, i].astype(BF16)
    all_ref[...] = ti_ref[...]

    row_at = [turned(k, halo, over) for k in range(halo)]
    own_halo = [[side_ref[turned(p, planes, core == 1), at] for at in row_at] for p in range(planes)]
    corner = [[corner_ref[turned(p, half, core == 1), at] for at in row_at] for p in range(half)]
    corner = [[jnp.where(ends, jnp.zeros_like(v), v) for v in pair_] for pair_ in corner]

    def pair(blocks):
        sides = []
        for start in range(2):
            flat = []
            for near, late in blocks:
                flat += near[start:] + late[: start + 1]
            sides.append(jnp.concatenate(flat, axis=0))
        return jnp.concatenate(sides, axis=1)

    def near(ref, p):
        return [ref[p, slot, :, right] for slot in (rows, rows + 1)]

    own_rows = [(near(xo_ref, p), own_halo[p]) for p in range(planes)]
    far_rows = [(near(xz_ref, p), corner[p]) for p in range(half)]
    late = [None] * (half + 2)

    def store(base):
        def put(p, a, b):
            late[base + p] = [a, b]

        return put

    w1 = w1_ref[...]
    first_layer(w1, pair(own_rows), half, chans, None, store(half))
    first_layer(w1, pair(far_rows + own_rows[:half]), half, chans, ends, store(0))
    x = pair(
        [
            ([ref[p, slot, :, right] for slot in (rows - 1, rows)], late[base + p])
            for base, ref in ((0, fz_ref), (half, fo_ref))
            for p in range(half)
        ]
    )
    two_rows = (2 * rows - 2, 2 * rows - 1)

    def put(far, at, feat):
        def mine():
            keep_ref[at] = feat

        def theirs():
            send_ref[pl.ds(pl.multiple_of(at * chans, chans), chans)] = feat.astype(BF16)

        pl.when(kept == far)(mine)
        pl.when(kept != far)(theirs)

    second_layer(w2_ref[...], x, pb_ref[...], ps_ref, fracs, two_rows, over, put, all_ref)
    stat_ref[...] = all_ref[kept]
    flat = stat_pieces(*[all_ref[given, k] for k in range(3)])
    send_ref[rows * chans :] = jnp.concatenate(flat, axis=0).astype(BF16)


def merge(one, two, rows):
    (feat_a, stats_a), (feat_b, stats_b) = one, two
    peak = jnp.maximum(stats_a[0], stats_b[0])
    wa = jnp.exp(stats_a[0] - peak)
    wb = jnp.exp(stats_b[0] - peak)
    total = wa * stats_a[1] + wb * stats_b[1]
    depth = wa * stats_a[2] + wb * stats_b[2]
    feats = [
        wa[i : i + 1] * feat_a(i) + wb[i : i + 1] * feat_b(i) for i in range(rows)
    ]
    return feats, peak, total, depth


def parcel(ref, rows):
    chans = ref.shape[0] // rows - STATS
    return (lambda i: ref[i * chans : (i + 1) * chans].astype(F32)), load_stats(ref, rows)


def first_merge_kernel(keep_ref, stat_ref, got_ref, out_ref):
    rows = keep_ref.shape[0]
    mine = (lambda i: keep_ref[i]), tuple(stat_ref[k] for k in range(3))
    store_parcel(out_ref, *merge(mine, parcel(got_ref, rows), rows))


def merge_group(step, refs, rows, finish):
    def go(me):
        parts = [parcel(refs[me ^ j], rows) for j in range(len(refs))]
        while True:
            merged = [merge(a, b, rows) for a, b in zip(parts[::2], parts[1::2])]
            if len(merged) == 1:
                return finish(*merged[0])
            parts = [(m[0].__getitem__, m[1:]) for m in merged]

    place = (lax.axis_index("depth") // step) & (len(refs) - 1)
    for me in range(len(refs)):
        pl.when(place == me)(functools.partial(go, me))


def merge_kernel(step, rows, *refs):
    merge_group(step, refs[:-1], rows, functools.partial(store_parcel, refs[-1]))


def last_merge_kernel(step, *refs):
    joined_ref, depth_ref = refs[-2:]
    rows = joined_ref.shape[0]

    def finish(feats, peak, total, depth):
        inverse = 1.0 / total
        for i in range(rows):
            joined_ref[i] = feats[i] * inverse[i : i + 1]
        depth_ref[...] = depth * inverse

    merge_group(step, refs[:-2], rows, finish)


def merge_rounds(depth):
    rounds = []
    step = 1
    while step < depth:
        count = 4 if step * 4 <= depth else 2
        rounds.append((step, count))
        step *= count
    return rounds


def call(kernel, outs, *args, scratch=(), flops=0, nbytes=0, room=4):
    return pl.pallas_call(
        kernel,
        out_shape=[jax.ShapeDtypeStruct(s, t) for s, t in outs],
        in_specs=[VMEM] * len(args),
        out_specs=[VMEM] * len(outs),
        scratch_shapes=list(scratch),
        cost_estimate=pl.CostEstimate(flops=flops, bytes_accessed=nbytes, transcendentals=0),
        compiler_params=pltpu.CompilerParams(vmem_limit_bytes=room * 2**20),
    )(*args)


def body(volume, prior, first_kernel, second_kernel, projection):
    planes, rows, chans, width = volume.shape
    depth, rows_axis = lax.axis_size("depth"), lax.axis_size("rows")
    shape = (depth, rows_axis)
    half = planes // 2
    halo = 2
    taps = first_kernel.shape[0]
    columns = rows_axis // 2
    assert half == halo and columns == 2 and rows_axis == 4 and depth & (depth - 1) == 0

    def move(value, target):
        return exchange(value, shape, target)

    weight_shape = (taps * half * chans, (half + 2) * taps * chans)
    w1, w2, pb = call(
        prepare_kernel,
        [(weight_shape, BF16), (weight_shape, BF16), ((chans, width), F32)],
        first_kernel, second_kernel, projection[None, :],
        flops=10**8, nbytes=10**6,
    )

    core = (lax.axis_index("rows") & 1)
    col = (lax.axis_index("rows") >> 1)
    lower = core == 0
    beside = move(volume, lambda d, r: (d, r ^ 1))
    prior_beside = move(prior, lambda d, r: (d, r ^ 1))
    beside, prior_beside = lax.optimization_barrier((beside, prior_beside))

    high = slice(0, halo)
    low = slice(rows - halo, rows)

    def parts(block):
        picked = jnp.where(lower, block[:half], block[half:])
        return picked, block[:, high], block[:, low]

    edge_shape = (planes, halo, chans, width)
    own_pick, own_high, own_low = call(
        cut_kernel,
        [((half, rows, chans, width), BF16), (edge_shape, BF16), (edge_shape, BF16)],
        volume,
    )
    sib_pick, sib_high, sib_low = parts(beside)
    edge = jnp.where(
        lower,
        jnp.concatenate([own_pick, sib_pick], axis=1),
        jnp.concatenate([sib_pick, own_pick], axis=1),
    )
    top_high = jnp.where(lower, own_high, sib_high)
    bottom_low = jnp.where(lower, sib_low, own_low)

    def up(d, r):
        to = d + 1 if r % 2 else d - 1
        return (to, r ^ 1) if 0 <= to < depth else (d, r ^ 2)

    def up_across(d, r):
        to = d + 1 if r % 2 else d - 1
        return (to, r ^ 3) if 0 <= to < depth else (d, r ^ 2)

    zh = move(edge, up)
    pay = jnp.where(col == 0, bottom_low, top_high)
    corner = jnp.where(lower, pay[:half], pay[half:])
    side = move(pay, lambda d, r: (d, r ^ 3))
    corner = move(corner, up_across)

    parcel_shape = (rows * (chans + STATS), width)
    stats_shape = (3, rows, width)
    block_shape = (planes, rows + 2, chans, 2 * width)
    xo, fo, ps = call(
        functools.partial(own_kernel, depth),
        [
            (block_shape, BF16),
            ((half, rows + 1, chans, 2 * width), BF16),
            ((2, half, rows, width), F32),
        ],
        volume, beside, prior, prior_beside, w1,
        flops=2 * 10**8, nbytes=10**6, room=6,
    )
    inside = call(
        functools.partial(inner_kernel, depth),
        [
            ((half, rows + 2, chans, 2 * width), BF16),
            ((half, rows + 1, chans, 2 * width), BF16),
            ((2, rows, chans, width), F32),
            ((2,) + stats_shape, F32),
        ],
        zh, xo, fo, ps, w1, w2, pb,
        flops=5 * 10**8, nbytes=10**6, room=6,
    )
    keep, stat, send = call(
        functools.partial(outer_kernel, depth),
        [((rows, chans, width), F32), (stats_shape, F32), (parcel_shape, BF16)],
        side, corner, xo, fo, ps, *inside, w1, w2, pb,
        scratch=[pltpu.VMEM((2,) + stats_shape, F32)],
        flops=10**8, nbytes=10**6, room=6,
    )
    got = move(send, lambda d, r: (d, r ^ 1))
    (sums,) = call(first_merge_kernel, [(parcel_shape, BF16)], keep, stat, got)
    rounds = merge_rounds(depth)
    for step, count in rounds:
        others = [move(sums, lambda d, r: (d ^ (k * step), r)) for k in range(1, count)]
        if (step, count) != rounds[-1]:
            (sums,) = call(
                functools.partial(merge_kernel, step, rows), [(parcel_shape, BF16)], sums, *others
            )
    joined, depth_estimate = call(
        functools.partial(last_merge_kernel, step),
        [((rows, chans, width), F32), ((rows, width), F32)],
        sums, *others,
    )
    return joined, depth_estimate


def solution(mesh):
    placed = (
        P(("tiles", "depth"), "rows", None, None),
        P(("tiles", "depth"), "rows", None),
        P(),
        P(),
        P(),
    )
    return jax.shard_map(
        body,
        mesh=mesh,
        in_specs=placed,
        out_specs=(P(("tiles", "rows"), None, None), P(("tiles", "rows"), None)),
        check_vma=False,
    )
```

```python
import functools

import jax
import jax.numpy as jnp
from jax import lax
from jax.experimental import pallas as pl
from jax.experimental.pallas import tpu as pltpu
from jax.sharding import PartitionSpec as P


F32 = jnp.float32
BF16 = jnp.bfloat16
AXES = ("depth", "rows")
STATS = 5
VMEM = pl.BlockSpec(memory_space=pltpu.VMEM)


def exchange(value, shape, target):
    depth, rows = shape
    pairs = []
    for d in range(depth):
        for r in range(rows):
            to_d, to_r = target(d, r)
            if 0 <= to_d < depth and 0 <= to_r < rows:
                pairs.append((d * rows + r, to_d * rows + to_r))
    return lax.ppermute(value, AXES, pairs)


def prepare_kernel(k1_ref, k2_ref, proj_ref, w1_ref, w2_ref, pb_ref):
    taps = k1_ref.shape[0]
    chans = k1_ref.shape[3]
    span = taps * chans
    turned_over = (lax.axis_index("rows") >> 1) == 1
    row_tap = [jnp.where(turned_over, taps - 1 - b, b) for b in range(taps)]
    upper = (lax.axis_index("rows") & 1) == 1
    plane_tap = [jnp.where(upper, taps - 1 - a, a) for a in range(taps)]
    for k_ref, w_ref in ((k1_ref, w1_ref), (k2_ref, w2_ref)):
        made = w_ref.shape[0] // (taps * chans)
        for e in range(taps):
            flat = jnp.concatenate(
                [k_ref[plane_tap[a], row_tap[b], e].astype(F32) for a in range(taps) for b in range(taps)]
                + [jnp.zeros(((made - 1) * span, chans), F32)],
                axis=0,
            )
            turned = flat.T
            for p in range(made):
                moved = turned if p == 0 else pltpu.roll(turned, p * span, 1)
                at = (e * made + p) * chans
                w_ref[at : at + chans, :] = moved.astype(BF16)
    lanes = pb_ref.shape[1]
    pb_ref[...] = jnp.broadcast_to(proj_ref[...], (lanes, chans)).T


def cut_kernel(block_ref, pick_ref, high_ref, low_ref):
    half, halo = pick_ref.shape[0], high_ref.shape[1]
    rows = block_ref.shape[1]
    core = (lax.axis_index("rows") & 1)
    pick_ref[...] = block_ref[pl.ds(core * half, half)]
    high_ref[...] = block_ref[:, :halo]
    low_ref[...] = block_ref[:, rows - halo :]


def shifted_sum(y, group):
    width = y.shape[1] // 2
    lane = lax.broadcasted_iota(jnp.int32, (1, width), 1)
    parts = []
    for s in range(2):
        cols = slice(s * width, (s + 1) * width)
        before = pltpu.roll(y[:group, cols], 1, 1)
        here = y[group : 2 * group, cols]
        after = pltpu.roll(y[2 * group :, cols], width - 1, 1)
        parts.append(
            here + jnp.where(lane == 0, 0.0, before) + jnp.where(lane == width - 1, 0.0, after)
        )
    return parts


def pieces(value, count):
    out = []
    for _ in range(count - 1):
        top = value.astype(BF16).astype(F32)
        out.append(top)
        value = value - top
    return out + [value]


def stat_pieces(peak, total, depth):
    return pieces(peak * 0.5, 3) + [total, depth]


def store_parcel(ref, feats, peak, total, depth):
    chans = feats[0].shape[0]
    for i, feat in enumerate(feats):
        ref[i * chans : (i + 1) * chans] = feat.astype(BF16)
    flat = stat_pieces(peak, total, depth)
    ref[len(feats) * chans :] = jnp.concatenate(flat, axis=0).astype(BF16)


def load_stats(ref, rows):
    flat = ref[ref.shape[0] - STATS * rows :].astype(F32)
    flat = [flat[k * rows : (k + 1) * rows] for k in range(STATS)]
    return ((flat[0] + flat[1]) + flat[2]) * 2.0, flat[3], flat[4]


def first_layer(w, x, half, chans, ends, store):
    lo, hi = shifted_sum(jnp.dot(w, x, preferred_element_type=F32), half * chans)
    for p in range(half):
        part = slice(p * chans, (p + 1) * chans)
        a, b = jnp.maximum(lo[part], 0.0), jnp.maximum(hi[part], 0.0)
        if ends is not None and p == 0:
            a = jnp.where(ends, 0.0, a)
            b = jnp.where(ends, 0.0, b)
        store(p, a.astype(BF16), b.astype(BF16))


def second_layer(w, x, pb, ps_ref, fracs, two_rows, over, put, stat_ref):
    chans = pb.shape[0]
    rows = ps_ref.shape[2]
    half = len(fracs)
    y = jnp.dot(w, x, preferred_element_type=F32)
    for row, side in zip(two_rows, shifted_sum(y, half * chans)):
        far = row // rows
        at = jnp.where(over, rows - 1 - row % rows, row % rows)
        side = jnp.maximum(side, 0.0).astype(BF16).astype(F32)
        feats = [side[p * chans : (p + 1) * chans] for p in range(half)]
        scores = [
            jnp.sum(feats[p] * pb, axis=0, keepdims=True) + ps_ref[far, p, pl.ds(at, 1), :]
            for p in range(half)
        ]
        peak = functools.reduce(jnp.maximum, scores)
        weights = [jnp.exp(s_ - peak) for s_ in scores]
        total = functools.reduce(jnp.add, weights)
        depth_sum = functools.reduce(jnp.add, [w_ * f for w_, f in zip(weights, fracs)])
        put(far, at, functools.reduce(jnp.add, [w_ * f for w_, f in zip(weights, feats)]))
        for k, value in enumerate((peak, total, depth_sum)):
            stat_ref[far, k, pl.ds(at, 1), :] = value


def place_of(depth, planes):
    half = planes // 2
    d = lax.axis_index("depth")
    core = lax.axis_index("rows") & 1
    over = (lax.axis_index("rows") >> 1) == 1
    plane = [d * planes + jnp.where(core == 1, planes - 1 - p, p) for p in range(half)]
    fracs = [(p.astype(F32) + 0.5) / (depth * planes) for p in plane]
    ends = d == jnp.where(core == 1, depth - 1, 0)
    return core, over, fracs, ends


def turned(p, planes, flag):
    return jnp.where(flag, planes - 1 - p, p)


def fill_rows(ref, p, source, rows, row_of):
    chans, width = ref.shape[2], ref.shape[3] // 2
    for cols, start in ((slice(0, width), -1), (slice(width, 2 * width), rows - 2)):
        for slot in range(rows + 2):
            row = start + slot
            if row < 0:
                ref[p, slot, :, cols] = jnp.zeros((chans, width), BF16)
            else:
                ref[p, slot, :, cols] = source(row_of(row))


def first_rows(w, x_of, half, rows, ends, fs_ref):
    chans, wide = fs_ref.shape[2:]
    left, right = slice(0, wide // 2), slice(wide // 2, wide)
    for p in range(half):
        fs_ref[p, 0, :, left] = jnp.zeros((chans, wide // 2), BF16)
    for i in range(rows):
        def store(p, a, b, i=i):
            fs_ref[p, i + 1, :, left] = a
            fs_ref[p, i + 1, :, right] = b
            if i == rows - 2:
                fs_ref[p, 0, :, right] = a

        first_layer(w, x_of(slice(i, i + 3)).reshape(-1, wide), half, chans, ends, store)


def own_kernel(depth, own_ref, sib_ref, op_ref, sp_ref, w1_ref, xo_ref, fo_ref, ps_ref):
    planes, rows, _, _ = own_ref.shape
    half = planes // 2
    core, over, _, _ = place_of(depth, planes)

    def fill(c, flip):
        blocks = (own_ref, sib_ref) if c == 0 else (sib_ref, own_ref)
        priors = (op_ref, sp_ref) if c == 0 else (sp_ref, op_ref)
        for p in range(planes):
            plane = planes - 1 - p if c else p
            fill_rows(
                xo_ref, p, lambda row: blocks[row // rows][plane, row % rows], rows,
                lambda row: 2 * rows - 1 - row if flip else row,
            )
            if p < half:
                for k in range(2):
                    ps_ref[k, p] = priors[1 - k if flip else k][plane]

    for c in range(2):
        for flip in (False, True):
            pl.when(jnp.logical_and(core == c, over == flip))(functools.partial(fill, c, flip))
    first_rows(w1_ref[...], lambda at: xo_ref[:, at], half, rows, None, fo_ref)


def inner_kernel(
    depth, zh_ref, xo_ref, fo_ref, ps_ref, w1_ref, w2_ref, pb_ref,
    xz_ref, fz_ref, feat_ref, stat_ref,
):
    half = zh_ref.shape[0]
    planes = xo_ref.shape[0]
    rows = xo_ref.shape[1] - 2
    wide = xo_ref.shape[3]
    lead = rows - 1
    core, over, fracs, ends = place_of(depth, planes)
    for p in range(half):
        plane = turned(p, half, core == 1)

        def source(row):
            got = zh_ref[plane, row]
            return jnp.where(ends, jnp.zeros_like(got), got)

        fill_rows(xz_ref, p, source, rows, lambda row: turned(row, 2 * rows, over))

    first_rows(
        w1_ref[...], lambda at: jnp.concatenate([xz_ref[:, at], xo_ref[:half, at]], axis=0),
        half, rows, ends, fz_ref,
    )

    def put(far, at, feat):
        feat_ref[far, at] = feat

    w2 = w2_ref[...]
    pb = pb_ref[...]
    for i in range(lead):
        at = slice(i, i + 3)
        x = jnp.concatenate([fz_ref[:, at], fo_ref[:, at]], axis=0).reshape(-1, wide)
        second_layer(w2, x, pb, ps_ref, fracs, (i, i + lead), over, put, stat_ref)


def outer_kernel(
    depth, side_ref, corner_ref, xo_ref, fo_ref, ps_ref, xz_ref, fz_ref, fi_ref, ti_ref, w1_ref,
    w2_ref, pb_ref, keep_ref, stat_ref, send_ref, all_ref,
):
    planes, halo, chans, width = side_ref.shape
    half = planes // 2
    rows = keep_ref.shape[0]
    core, over, fracs, ends = place_of(depth, planes)
    right = slice(width, 2 * width)
    kept = jnp.where(over, 1 - core, core)
    given = 1 - kept
    keep_ref[...] = fi_ref[kept]
    for i in range(rows):
        send_ref[i * chans : (i + 1) * chans] = fi_ref[given, i].astype(BF16)
    all_ref[...] = ti_ref[...]

    row_at = [turned(k, halo, over) for k in range(halo)]
    own_halo = [[side_ref[turned(p, planes, core == 1), at] for at in row_at] for p in range(planes)]
    corner = [[corner_ref[turned(p, half, core == 1), at] for at in row_at] for p in range(half)]
    corner = [[jnp.where(ends, jnp.zeros_like(v), v) for v in pair_] for pair_ in corner]

    def pair(blocks):
        sides = []
        for start in range(2):
            flat = []
            for near, late in blocks:
                flat += near[start:] + late[: start + 1]
            sides.append(jnp.concatenate(flat, axis=0))
        return jnp.concatenate(sides, axis=1)

    def near(ref, p):
        return [ref[p, slot, :, right] for slot in (rows, rows + 1)]

    own_rows = [(near(xo_ref, p), own_halo[p]) for p in range(planes)]
    far_rows = [(near(xz_ref, p), corner[p]) for p in range(half)]
    late = [None] * (half + 2)

    def store(base):
        def put(p, a, b):
            late[base + p] = [a, b]

        return put

    w1 = w1_ref[...]
    first_layer(w1, pair(own_rows), half, chans, None, store(half))
    first_layer(w1, pair(far_rows + own_rows[:half]), half, chans, ends, store(0))
    x = pair(
        [
            ([ref[p, slot, :, right] for slot in (rows - 1, rows)], late[base + p])
            for base, ref in ((0, fz_ref), (half, fo_ref))
            for p in range(half)
        ]
    )
    two_rows = (2 * rows - 2, 2 * rows - 1)

    def put(far, at, feat):
        def mine():
            keep_ref[at] = feat

        def theirs():
            send_ref[pl.ds(pl.multiple_of(at * chans, chans), chans)] = feat.astype(BF16)

        pl.when(kept == far)(mine)
        pl.when(kept != far)(theirs)

    second_layer(w2_ref[...], x, pb_ref[...], ps_ref, fracs, two_rows, over, put, all_ref)
    stat_ref[...] = all_ref[kept]
    flat = stat_pieces(*[all_ref[given, k] for k in range(3)])
    send_ref[rows * chans :] = jnp.concatenate(flat, axis=0).astype(BF16)


def merge(one, two, rows):
    (feat_a, stats_a), (feat_b, stats_b) = one, two
    peak = jnp.maximum(stats_a[0], stats_b[0])
    wa = jnp.exp(stats_a[0] - peak)
    wb = jnp.exp(stats_b[0] - peak)
    total = wa * stats_a[1] + wb * stats_b[1]
    depth = wa * stats_a[2] + wb * stats_b[2]
    feats = [
        wa[i : i + 1] * feat_a(i) + wb[i : i + 1] * feat_b(i) for i in range(rows)
    ]
    return feats, peak, total, depth


def parcel(ref, rows):
    chans = ref.shape[0] // rows - STATS
    return (lambda i: ref[i * chans : (i + 1) * chans].astype(F32)), load_stats(ref, rows)


def first_merge_kernel(keep_ref, stat_ref, got_ref, out_ref):
    rows = keep_ref.shape[0]
    mine = (lambda i: keep_ref[i]), tuple(stat_ref[k] for k in range(3))
    store_parcel(out_ref, *merge(mine, parcel(got_ref, rows), rows))


def partner(core, k, count):
    return (((2, 3, 1), (2, 1, 3))[core][k - 1]) if count == 4 else k


def merge_group(step, refs, rows, finish):
    def go(me, core):
        at = [0] * len(refs)
        for k in range(1, len(refs)):
            at[partner(core, k, len(refs))] = k
        parts = [parcel(refs[at[me ^ j]], rows) for j in range(len(refs))]
        while True:
            merged = [merge(a, b, rows) for a, b in zip(parts[::2], parts[1::2])]
            if len(merged) == 1:
                return finish(*merged[0])
            parts = [(m[0].__getitem__, m[1:]) for m in merged]

    place = (lax.axis_index("depth") // step) & (len(refs) - 1)
    core = lax.axis_index("rows") & 1
    for me in range(len(refs)):
        for c in range(2):
            pl.when(jnp.logical_and(place == me, core == c))(functools.partial(go, me, c))


def merge_kernel(step, rows, *refs):
    merge_group(step, refs[:-1], rows, functools.partial(store_parcel, refs[-1]))


def last_merge_kernel(step, *refs):
    joined_ref, depth_ref = refs[-2:]
    rows = joined_ref.shape[0]

    def finish(feats, peak, total, depth):
        inverse = 1.0 / total
        for i in range(rows):
            joined_ref[i] = feats[i] * inverse[i : i + 1]
        depth_ref[...] = depth * inverse

    merge_group(step, refs[:-2], rows, finish)


def merge_rounds(depth):
    rounds = []
    step = 1
    while step < depth:
        count = 4 if step * 4 <= depth else 2
        rounds.append((step, count))
        step *= count
    return rounds


def call(kernel, outs, *args, scratch=(), flops=0, nbytes=0, room=4):
    return pl.pallas_call(
        kernel,
        out_shape=[jax.ShapeDtypeStruct(s, t) for s, t in outs],
        in_specs=[VMEM] * len(args),
        out_specs=[VMEM] * len(outs),
        scratch_shapes=list(scratch),
        cost_estimate=pl.CostEstimate(flops=flops, bytes_accessed=nbytes, transcendentals=0),
        compiler_params=pltpu.CompilerParams(vmem_limit_bytes=room * 2**20),
    )(*args)


def body(volume, prior, first_kernel, second_kernel, projection):
    planes, rows, chans, width = volume.shape
    depth, rows_axis = lax.axis_size("depth"), lax.axis_size("rows")
    shape = (depth, rows_axis)
    half = planes // 2
    halo = 2
    taps = first_kernel.shape[0]
    columns = rows_axis // 2
    assert half == halo and columns == 2 and rows_axis == 4 and depth & (depth - 1) == 0

    def move(value, target):
        return exchange(value, shape, target)

    weight_shape = (taps * half * chans, (half + 2) * taps * chans)
    w1, w2, pb = call(
        prepare_kernel,
        [(weight_shape, BF16), (weight_shape, BF16), ((chans, width), F32)],
        first_kernel, second_kernel, projection[None, :],
        flops=10**8, nbytes=10**6,
    )

    core = (lax.axis_index("rows") & 1)
    col = (lax.axis_index("rows") >> 1)
    lower = core == 0
    beside = move(volume, lambda d, r: (d, r ^ 1))
    prior_beside = move(prior, lambda d, r: (d, r ^ 1))
    beside, prior_beside = lax.optimization_barrier((beside, prior_beside))

    high = slice(0, halo)
    low = slice(rows - halo, rows)

    def parts(block):
        picked = jnp.where(lower, block[:half], block[half:])
        return picked, block[:, high], block[:, low]

    edge_shape = (planes, halo, chans, width)
    own_pick, own_high, own_low = call(
        cut_kernel,
        [((half, rows, chans, width), BF16), (edge_shape, BF16), (edge_shape, BF16)],
        volume,
    )
    sib_pick, sib_high, sib_low = parts(beside)
    edge = jnp.where(
        lower,
        jnp.concatenate([own_pick, sib_pick], axis=1),
        jnp.concatenate([sib_pick, own_pick], axis=1),
    )
    top_high = jnp.where(lower, own_high, sib_high)
    bottom_low = jnp.where(lower, sib_low, own_low)

    def up(d, r):
        to = d + 1 if r % 2 else d - 1
        return (to, r ^ 1) if 0 <= to < depth else (d, r ^ 2)

    def up_across(d, r):
        to = d + 1 if r % 2 else d - 1
        return (to, r ^ 3) if 0 <= to < depth else (d, r ^ 2)

    zh = move(edge, up)
    pay = jnp.where(col == 0, bottom_low, top_high)
    corner = jnp.where(lower, pay[:half], pay[half:])
    side = move(pay, lambda d, r: (d, r ^ 3))
    corner = move(corner, up_across)

    parcel_shape = (rows * (chans + STATS), width)
    stats_shape = (3, rows, width)
    block_shape = (planes, rows + 2, chans, 2 * width)
    xo, fo, ps = call(
        functools.partial(own_kernel, depth),
        [
            (block_shape, BF16),
            ((half, rows + 1, chans, 2 * width), BF16),
            ((2, half, rows, width), F32),
        ],
        volume, beside, prior, prior_beside, w1,
        flops=2 * 10**8, nbytes=10**6, room=6,
    )
    inside = call(
        functools.partial(inner_kernel, depth),
        [
            ((half, rows + 2, chans, 2 * width), BF16),
            ((half, rows + 1, chans, 2 * width), BF16),
            ((2, rows, chans, width), F32),
            ((2,) + stats_shape, F32),
        ],
        zh, xo, fo, ps, w1, w2, pb,
        flops=5 * 10**8, nbytes=10**6, room=6,
    )
    keep, stat, send = call(
        functools.partial(outer_kernel, depth),
        [((rows, chans, width), F32), (stats_shape, F32), (parcel_shape, BF16)],
        side, corner, xo, fo, ps, *inside, w1, w2, pb,
        scratch=[pltpu.VMEM((2,) + stats_shape, F32)],
        flops=10**8, nbytes=10**6, room=6,
    )
    got = move(send, lambda d, r: (d, r ^ 1))
    (sums,) = call(first_merge_kernel, [(parcel_shape, BF16)], keep, stat, got)
    rounds = merge_rounds(depth)
    for step, count in rounds:
        others = [
            move(sums, lambda d, r: (d ^ (partner(r & 1, k, count) * step), r))
            for k in range(1, count)
        ]
        if (step, count) != rounds[-1]:
            (sums,) = call(
                functools.partial(merge_kernel, step, rows), [(parcel_shape, BF16)], sums, *others
            )
    joined, depth_estimate = call(
        functools.partial(last_merge_kernel, step),
        [((rows, chans, width), F32), ((rows, width), F32)],
        sums, *others,
    )
    return joined, depth_estimate


def solution(mesh):
    placed = (
        P(("tiles", "depth"), "rows", None, None),
        P(("tiles", "depth"), "rows", None),
        P(),
        P(),
        P(),
    )
    return jax.shard_map(
        body,
        mesh=mesh,
        in_specs=placed,
        out_specs=(P(("tiles", "rows"), None, None), P(("tiles", "rows"), None)),
        check_vma=False,
    )
```
